512 devices in a mesh: cell: 128 (over z, y, core), tm: 4 (over x).
Axes of the slice: x: 4, y: 8, z: 8, core: 2. Of those that a mesh axis runs over, the one named last changes fastest.
Arguments:
- snapshots: float32 [384, 5, 98304], P('tm', None, 'cell'), may hold values from -6 to 6
- volumes: float32 [98304], P('cell'), may hold values from 0.1 to 10
- freq_index: int32 [8], replicated, may hold values from 1 to 63, as said below
- block_start: int32 [5], replicated, may hold values from 0 to 256, as said below
Outputs:
- modes: float32 [8, 10, 5, 98304], P('tm', None, None, 'cell')
- triangle: float32 [8, 10, 10], P('tm')
The draws below stay inside these ranges and needn't reach their ends.
Inputs may be any that keep to these rules, and one draw needn't show every extreme that they name: `freq_index`: distinct indices; the smallest and the largest allowed value both occur. `block_start`: rising; the first is 0 and the last is 256; with s = 64, start b lies within s // 4 of b * s.
All inputs are finite; a program needn't handle non-finite values.
Results may differ from the reference program's by a relative error of at most 0.000078.
Values sent between devices are 32-bit elements; how exact they have to be, the bound alone decides.
No kernel may reach another device: no remote copies, remote signals or barrier semaphores. Data moves between devices by JAX's collectives and lax.ppermute only.
A program may use at most 64 MiB of HBM per device.

```python
import math
import jax
import jax.numpy as jnp
from jax import lax

V = 5
NFFT = 128
NF = 8
NB = 5
TSNAP = 384
NCELL = 98304


def draw_freq_index(key, part):
    picked = jax.random.permutation(key, NFFT // 2 - 3)[:NF - 2].astype(jnp.int32) + 2
    return jnp.concatenate([jnp.array([1], jnp.int32), picked, jnp.array([NFFT // 2 - 1], jnp.int32)])


def draw_block_start(key, part):
    step_size = (TSNAP - NFFT) // (NB - 1)
    jitter_most = step_size // 4
    jitter = jax.random.randint(key, (NB - 2,), -jitter_most, jitter_most + 1).astype(jnp.int32)
    middle = (jnp.arange(1, NB - 1, dtype=jnp.int32) * step_size + jitter).astype(jnp.int32)
    return jnp.concatenate([jnp.array([0], jnp.int32), middle, jnp.array([TSNAP - NFFT], jnp.int32)])


def block_levels(stream_key, shape, shards, least, largest):
    def one(position, parts):
        steps = jax.random.uniform(jax.random.fold_in(jax.random.fold_in(stream_key, 6), position), (parts,), jnp.float32, least / len(shards), largest / len(shards))
        return jnp.repeat(jnp.exp(steps), shape[position] // parts).reshape((-1,) + (1,) * (len(shape) - position - 1))

    factor_of = one(*shards[0])
    for cut in shards[1:]:
        factor_of = factor_of * one(*cut)
    return factor_of


def normal_values(rng, shape, deviation, bound, shards=(), held_as=jnp.bfloat16):
    drawn = deviation * jax.random.normal(rng, shape, jnp.float32)
    if shards:
        drawn = drawn * block_levels(rng, shape, shards, -0.22, 0.18)
    return jnp.clip(drawn, -bound, bound).astype(held_as)


def setup_inputs(seed: int = 0) -> dict:
    key_list = jax.random.split(jax.random.key(seed), 5)
    snapshots = normal_values(key_list[0], (TSNAP, V, NCELL), 1.0, 6.0, ((0, 4), (2, 128)), jnp.float32)
    volumes = jnp.clip(jnp.exp(math.log(10.0) - 4.6051702 * jax.random.uniform(key_list[1], (NCELL,), jnp.float32) ** block_levels(key_list[1], (NCELL,), ((0, 128),), -0.2, 0.2)), 0.1, 10.0)
    freq_index = draw_freq_index(jax.random.fold_in(key_list[4], 71), 0)
    block_start = draw_block_start(jax.random.fold_in(key_list[4], 71), 0)
    return {"snapshots": snapshots, "volumes": volumes, "freq_index": freq_index, "block_start": block_start}


def make_table(freq_index, block_start, times):
    tau = times[None, :] - block_start[:, None]
    valid = (tau >= 0) & (tau < NFFT)
    tauf = tau.astype(jnp.float32)
    hann = jnp.where(valid, 0.5 - 0.5 * jnp.cos(2.0 * jnp.pi * tauf / NFFT), 0.0)
    phase = jnp.mod(freq_index[:, None, None] * tau[None, :, :], NFFT).astype(jnp.float32)
    angle = 2.0 * jnp.pi * phase / NFFT
    real_part = hann[None] * jnp.cos(angle)
    imag_part = -hann[None] * jnp.sin(angle)
    table = jnp.stack([real_part, imag_part], axis=1)
    return table.reshape(NF * 2 * NB, times.shape[0]).astype(jnp.float32)

def reference(snapshots, volumes, freq_index, block_start):
    times = jnp.arange(TSNAP, dtype=jnp.int32)
    table = make_table(freq_index, block_start, times)
    flat = snapshots.reshape(TSNAP, V * NCELL)
    spectra = jnp.dot(table.astype(jnp.float32), flat.astype(jnp.float32), precision=lax.Precision.HIGHEST, preferred_element_type=jnp.float32)
    spectra = spectra.reshape(NF, 2 * NB, V, NCELL)
    weighted = spectra * jnp.sqrt(volumes)[None, None, None, :]
    weighted = weighted.reshape(NF, 2 * NB, V * NCELL)
    gram = jnp.einsum('frc,fsc->frs', weighted, weighted, precision=lax.Precision.HIGHEST)
    lower = jnp.linalg.cholesky(gram)
    solved = jax.vmap(lambda a, b: jax.scipy.linalg.solve_triangular(a, b, lower=True))(lower, weighted)
    modes = (jnp.sqrt(jnp.float32(V * NCELL)) * solved).reshape(NF, 2 * NB, V, NCELL)
    triangle = jnp.transpose(lower, (0, 2, 1)) / jnp.sqrt(jnp.float32(V * NCELL * NFFT))
    return (modes, triangle)
```

```python
import functools

import jax
import jax.numpy as jnp
from jax import lax
from jax.experimental import pallas as pl
from jax.experimental.pallas import tpu as pltpu
from jax.sharding import PartitionSpec as P

NFFT = 128
NF = 8
NB = 5
COLS = 2 * NB
SLOTS = NB - 1
TWO_PI = 6.283185307179586


def pieces(x):
    high = x.astype(jnp.bfloat16)
    rest = x - high.astype(jnp.float32)
    middle = rest.astype(jnp.bfloat16)
    low = (rest - middle.astype(jnp.float32)).astype(jnp.bfloat16)
    return high, middle, low


def dot(a, b, contract=((1,), (0,))):
    return lax.dot_general(a, b, (contract, ((), ())), preferred_element_type=jnp.float32)


def transform_kernel(freq_ref, start_ref, x_ref, out_ref, table_ref):
    tdev = x_ref.shape[1]
    cells = x_ref.shape[2]

    @pl.when(pl.program_id(0) == 0)
    def _():
        quarter = lax.axis_index("tm")
        first = jnp.where(quarter >= 2, 1, 0)
        sub = lax.broadcasted_iota(jnp.int32, (8, tdev), 0)
        time = lax.broadcasted_iota(jnp.int32, (8, tdev), 1) + quarter * tdev
        slot = sub % SLOTS
        start = jnp.zeros((8, tdev), jnp.int32)
        for s in range(SLOTS):
            start = jnp.where(slot == s, start_ref[first + s], start)
        tau = time - start
        valid = (tau >= 0) & (tau < NFFT)
        hann = jnp.where(valid, 0.5 - 0.5 * jnp.cos(TWO_PI / NFFT * tau.astype(jnp.float32)), 0.0)
        turn = jnp.where(sub >= SLOTS, NFFT // 4, 0)
        rows = []
        for g in range(NF):
            phase = (freq_ref[g] * tau + turn) & (NFFT - 1)
            rows.append(hann * jnp.cos(TWO_PI / NFFT * phase.astype(jnp.float32)))
        table = jnp.concatenate(rows, axis=0)
        high, middle, low = pieces(table)
        table_ref[0] = high
        table_ref[1] = middle
        table_ref[2] = low

    a0, a1, a2 = table_ref[0], table_ref[1], table_ref[2]
    x0, x1, x2 = pieces(x_ref[0])
    total = dot(a0, x2) + dot(a2, x0) + dot(a1, x1)
    total = total + dot(a0, x1) + dot(a1, x0)
    total = total + dot(a0, x0)
    out_ref[...] = total.reshape(4, 2 * COLS - 4, cells)


def transform(snapshots, freq_index, block_start):
    tdev, nvar, cells = snapshots.shape
    x = jnp.transpose(snapshots, (1, 0, 2))
    return pl.pallas_call(
        transform_kernel,
        grid=(nvar,),
        out_shape=jax.ShapeDtypeStruct((4, 16, nvar * cells), jnp.float32),
        in_specs=[
            pl.BlockSpec(memory_space=pltpu.SMEM),
            pl.BlockSpec(memory_space=pltpu.SMEM),
            pl.BlockSpec((1, tdev, cells), lambda v: (v, 0, 0)),
        ],
        out_specs=pl.BlockSpec((4, 16, cells), lambda v: (0, 0, v)),
        scratch_shapes=[pltpu.VMEM((3, 64, tdev), jnp.bfloat16)],
        name="transform",
    )(freq_index, block_start, x)


def gram_kernel(parts_ref, vol_ref, stack_ref, packed_ref):
    width = parts_ref.shape[2]
    nvar = width // vol_ref.shape[1]
    root = jnp.sqrt(vol_ref[...])
    root = jnp.concatenate([root] * nvar, axis=1)
    sub = lax.broadcasted_iota(jnp.int32, (8, width), 0)
    tiles = []
    for f in range(2):
        rows = slice(8 * f, 8 * f + 8)
        early = parts_ref[0, rows, :] + parts_ref[1, rows, :]
        late = parts_ref[2, rows, :] + parts_ref[3, rows, :]
        early1 = pltpu.roll(early, 1, 0)
        late1 = pltpu.roll(late, 1, 0)
        late2 = pltpu.roll(late, 2, 0)
        upper = jnp.where(sub < 4, early, jnp.where(sub >= 5, early1, 0.0))
        upper = upper + jnp.where((sub >= 1) & (sub < 5), late1, jnp.where(sub >= 6, late2, 0.0))
        lower = jnp.where(sub < 1, early1, 0.0) + jnp.where(sub < 2, late2, 0.0)
        tiles += [upper * root, lower * root]
    weighted = jnp.concatenate(tiles, axis=0)
    stack = jnp.concatenate(pieces(weighted), axis=0)
    stack_ref[...] = stack
    full = dot(stack, stack, ((1,), (1,)))
    full = full[0:32] + full[32:64] + full[64:96]
    full = full[:, 0:32] + full[:, 32:64] + full[:, 64:96]
    full = jnp.concatenate([full, jnp.zeros((32, 96), jnp.float32)], axis=1)
    row = lax.broadcasted_iota(jnp.int32, (16, 128), 0)
    lane = lax.broadcasted_iota(jnp.int32, (16, 128), 1)
    both = jnp.where(lane <= row, full[0:16], pltpu.roll(full[16:32], 128 - 15, 1))
    both = jnp.where((row < COLS) & (lane <= COLS), both, 0.0)
    moved = jnp.zeros((8, 128), jnp.float32)
    for i in range(COLS):
        tile = both[0:8] if i < 8 else both[8:16]
        tile = jnp.where(row[0:8] == i % 8, tile, 0.0)
        moved = moved + (pltpu.roll(tile, i * (COLS + 1), 1) if i else tile)
    packed_ref[...] = jnp.broadcast_to(jnp.sum(moved, axis=0, keepdims=True), packed_ref.shape)


def modes_kernel(rows_total, gram_ref, stack_ref, modes_ref, triangle_ref, inverse_ref, upper_ref):
    nvar = modes_ref.shape[1]
    cells = modes_ref.shape[3]
    total = jnp.sum(gram_ref[...], axis=0, keepdims=True)
    row = lax.broadcasted_iota(jnp.int32, (16, 128), 0)
    lane = lax.broadcasted_iota(jnp.int32, (16, 128), 1)
    total = jnp.broadcast_to(total, (8, 128))
    spread = [jnp.zeros((8, 128), jnp.float32)] * 2
    for i in range(COLS):
        moved = pltpu.roll(total, 128 - i * (COLS + 1), 1) if i else total
        spread[i // 8] = jnp.where(row[0:8] == i % 8, moved, spread[i // 8])
    spread = jnp.concatenate(spread, axis=0)
    first = jnp.where((lane <= row) & (row < COLS), spread, 0.0)
    first = jnp.transpose(jnp.concatenate([first, jnp.zeros((112, 128), jnp.float32)], axis=0))[0:16]
    second = pltpu.roll(spread, 127, 1)
    second = jnp.where((lane >= row) & (lane < COLS), second, 0.0)
    eye = jnp.where(lane == row + 16, 1.0, 0.0)
    for f, a in enumerate((first, second)):
        a = a + eye
        pivots = jnp.ones((16, 128), jnp.float32)
        for k in range(COLS):
            pivot_row = jnp.broadcast_to(a[k : k + 1, :], (16, 128))
            pivot = jnp.broadcast_to(a[k : k + 1, k : k + 1], (16, 128))
            pivots = jnp.where(row == k, pivot, pivots)
            if k < COLS - 1:
                column = jnp.sum(jnp.where(lane == row, pivot_row, 0.0), axis=1, keepdims=True)
                factor = jnp.where(row > k, column / pivot, 0.0)
                a = a - factor * pivot_row
        scale = 1.0 / jnp.sqrt(pivots)
        a = a * scale
        inverse = jnp.where((lane >= 16) & (lane < 32), a, 0.0)
        inverse = inverse if f else pltpu.roll(inverse, 128 - 16, 1)
        inverse_ref[pl.ds(f, 16, stride=2), :] = inverse * jnp.sqrt(jnp.float32(rows_total))
        upper_ref[pl.ds(f, 16, stride=2), :] = jnp.where(lane >= row, a, 0.0)
    inverse = inverse_ref[...]
    inverse = inverse + pltpu.roll(inverse, 32, 1) + pltpu.roll(inverse, 64, 1)
    left = jnp.concatenate([x[:, 0:96] for x in pieces(inverse)], axis=0)
    tri = upper_ref[...] / jnp.sqrt(jnp.float32(rows_total * NFFT))
    for j in range(COLS):
        triangle_ref[j] = tri[2 * j : 2 * j + 2, 0:COLS]
    for v in range(nvar):
        x = dot(left, stack_ref[:, v * cells : (v + 1) * cells])
        x = x[64:96] + x[32:64] + x[0:32]
        for j in range(COLS):
            modes_ref[j, v] = x[2 * j : 2 * j + 2, :]


def on_device(snapshots, volumes, freq_index, block_start):
    tdev, nvar, cells = snapshots.shape
    cell_count = lax.axis_size("cell")
    width = nvar * cells
    parts = transform(snapshots, freq_index, block_start)
    parts = lax.all_to_all(parts, "tm", 0, 0, tiled=True)
    stack, packed = pl.pallas_call(
        gram_kernel,
        out_shape=(
            jax.ShapeDtypeStruct((96, width), jnp.bfloat16),
            jax.ShapeDtypeStruct((cell_count, 128), jnp.float32),
        ),
        name="gram",
    )(parts, volumes.reshape(1, cells))
    shares = lax.all_to_all(packed, "cell", 0, 0, tiled=True)
    modes, triangle = pl.pallas_call(
        functools.partial(modes_kernel, width * cell_count),
        out_shape=(
            jax.ShapeDtypeStruct((COLS, nvar, 2, cells), jnp.float32),
            jax.ShapeDtypeStruct((COLS, 2, COLS), jnp.float32),
        ),
        scratch_shapes=[pltpu.VMEM((32, 128), jnp.float32), pltpu.VMEM((32, 128), jnp.float32)],
        name="modes",
    )(shares, stack)
    return jnp.transpose(modes, (2, 0, 1, 3)), jnp.transpose(triangle, (1, 0, 2))


def solution(mesh):
    placed = (P("tm", None, "cell"), P("cell"), P(), P())
    return jax.shard_map(
        on_device,
        mesh=mesh,
        in_specs=placed,
        out_specs=(P("tm", None, None, "cell"), P("tm", None, None)),
        check_vma=False,
    )
```

```python
import functools

import jax
import jax.numpy as jnp
from jax import lax
from jax.experimental import pallas as pl
from jax.experimental.pallas import tpu as pltpu
from jax.sharding import PartitionSpec as P

NFFT = 128
NF = 8
NB = 5
COLS = 2 * NB
SLOTS = NB - 1
TWO_PI = 6.283185307179586


def pieces(x):
    high = x.astype(jnp.bfloat16)
    rest = x - high.astype(jnp.float32)
    middle = rest.astype(jnp.bfloat16)
    low = (rest - middle.astype(jnp.float32)).astype(jnp.bfloat16)
    return high, middle, low


def dot(a, b, contract=((1,), (0,))):
    return lax.dot_general(a, b, (contract, ((), ())), preferred_element_type=jnp.float32)


def transform_kernel(freq_ref, start_ref, x_hbm, out_hbm, x_ref, out_ref, table_ref, in_sem, out_sem):
    nvar, tdev, cells = x_hbm.shape
    for v in range(nvar):
        pltpu.make_async_copy(x_hbm.at[v], x_ref.at[v], in_sem.at[v]).start()
    quarter = lax.axis_index("tm")
    first = jnp.where(quarter >= 2, 1, 0)
    sub = lax.broadcasted_iota(jnp.int32, (8, tdev), 0)
    time = lax.broadcasted_iota(jnp.int32, (8, tdev), 1) + quarter * tdev
    slot = sub % SLOTS
    start = jnp.zeros((8, tdev), jnp.int32)
    for s in range(SLOTS):
        start = jnp.where(slot == s, start_ref[first + s], start)
    tau = time - start
    valid = (tau >= 0) & (tau < NFFT)
    hann = jnp.where(valid, 0.5 - 0.5 * jnp.cos(TWO_PI / NFFT * tau.astype(jnp.float32)), 0.0)
    turn = jnp.where(sub >= SLOTS, NFFT // 4, 0)
    rows = []
    for g in range(NF):
        phase = (freq_ref[g] * tau + turn) & (NFFT - 1)
        rows.append(hann * jnp.cos(TWO_PI / NFFT * phase.astype(jnp.float32)))
    high, middle, low = pieces(jnp.concatenate(rows, axis=0))
    table_ref[:, 0:tdev] = jnp.concatenate([high, middle, low], axis=0)
    table_ref[:, tdev : 2 * tdev] = jnp.concatenate([high, middle, jnp.zeros_like(low)], axis=0)
    for v in range(nvar):
        at = slice(v * cells, (v + 1) * cells)
        pltpu.make_async_copy(x_hbm.at[v], x_ref.at[v], in_sem.at[v]).wait()
        x0, x1, x2 = pieces(x_ref[v])
        last = dot(table_ref[0:64, 0:tdev], x2)
        total = dot(table_ref[...], jnp.concatenate([x0, x1], axis=0))
        total = total[0:64] + (total[64:128] + (total[128:192] + last))
        out_ref[:, :, at] = total.reshape(4, 16, cells)
        pltpu.make_async_copy(out_ref.at[:, :, at], out_hbm.at[:, :, at], out_sem.at[v]).start()
    for v in range(nvar):
        at = slice(v * cells, (v + 1) * cells)
        pltpu.make_async_copy(out_ref.at[:, :, at], out_hbm.at[:, :, at], out_sem.at[v]).wait()


def transform(snapshots, freq_index, block_start):
    tdev, nvar, cells = snapshots.shape
    x = jnp.transpose(snapshots, (1, 0, 2))
    return pl.pallas_call(
        transform_kernel,
        out_shape=jax.ShapeDtypeStruct((4, 16, nvar * cells), jnp.float32),
        in_specs=[
            pl.BlockSpec(memory_space=pltpu.SMEM),
            pl.BlockSpec(memory_space=pltpu.SMEM),
            pl.BlockSpec(memory_space=pl.ANY),
        ],
        out_specs=pl.BlockSpec(memory_space=pl.ANY),
        scratch_shapes=[
            pltpu.VMEM((nvar, tdev, cells), jnp.float32),
            pltpu.VMEM((4, 16, nvar * cells), jnp.float32),
            pltpu.VMEM((192, 2 * tdev), jnp.bfloat16),
            pltpu.SemaphoreType.DMA((nvar,)),
            pltpu.SemaphoreType.DMA((nvar,)),
        ],
        name="transform",
    )(freq_index, block_start, x)


def gram_kernel(parts_ref, vol_ref, stack_ref, packed_ref):
    cells = vol_ref.shape[1]
    root = jnp.broadcast_to(jnp.sqrt(vol_ref[...]), (8, cells))
    sub = lax.broadcasted_iota(jnp.int32, (8, cells), 0)
    full = jnp.zeros((96, 96), jnp.float32)
    for v in range(parts_ref.shape[2] // cells):
        at = slice(v * cells, (v + 1) * cells)
        tiles = []
        for f in range(2):
            rows = slice(8 * f, 8 * f + 8)
            early = parts_ref[0, rows, at] + parts_ref[1, rows, at]
            late = parts_ref[2, rows, at] + parts_ref[3, rows, at]
            early1 = pltpu.roll(early, 1, 0)
            late1 = pltpu.roll(late, 1, 0)
            late2 = pltpu.roll(late, 2, 0)
            upper = jnp.where(sub < 4, early, jnp.where(sub >= 5, early1, 0.0))
            upper = upper + jnp.where((sub >= 1) & (sub < 5), late1, jnp.where(sub >= 6, late2, 0.0))
            lower = jnp.where(sub < 1, early1, 0.0) + jnp.where(sub < 2, late2, 0.0)
            tiles += [upper * root, lower * root]
        stack = jnp.concatenate(pieces(jnp.concatenate(tiles, axis=0)), axis=0)
        stack_ref[:, at] = stack
        full = full + dot(stack, stack, ((1,), (1,)))
    full = full[0:32] + full[32:64] + full[64:96]
    full = full[:, 0:32] + full[:, 32:64] + full[:, 64:96]
    full = jnp.concatenate([full, jnp.zeros((32, 96), jnp.float32)], axis=1)
    row = lax.broadcasted_iota(jnp.int32, (8, 128), 0)
    lane = lax.broadcasted_iota(jnp.int32, (8, 128), 1)
    moved = jnp.zeros((8, 128), jnp.float32)
    for f in range(2):
        for i in range(COLS):
            at = 16 * f + i // 8 * 8
            tile = jnp.where((row == i % 8) & (lane >= 16 * f) & (lane <= 16 * f + i), full[at : at + 8], 0.0)
            shift = 48 * f + i * (i + 1) // 2
            moved = moved + (pltpu.roll(tile, shift, 1) if shift else tile)
    packed_ref[...] = jnp.broadcast_to(jnp.sum(moved, axis=0, keepdims=True), packed_ref.shape)


def gram(parts, volumes, cell_count):
    width = parts.shape[2]
    return pl.pallas_call(
        gram_kernel,
        out_shape=(
            jax.ShapeDtypeStruct((96, width), jnp.bfloat16),
            jax.ShapeDtypeStruct((cell_count, 128), jnp.float32),
        ),
        compiler_params=pltpu.CompilerParams(vmem_limit_bytes=12 << 20),
        name="gram",
    )(parts, volumes.reshape(1, volumes.shape[0]))


def modes_kernel(rows_total, gram_ref, stack_ref, modes_hbm, triangle_ref, modes_ref, entry_ref, left_ref, sem):
    nvar = modes_ref.shape[1]
    cells = modes_ref.shape[3]
    total = jnp.broadcast_to(jnp.sum(gram_ref[...], axis=0, keepdims=True), (128, 128))
    total = jnp.transpose(total)
    entry_ref[...] = jnp.where(lax.broadcasted_iota(jnp.int32, (64, 128), 1) < 64, total[0:64], total[64:128])
    a = {}
    for i in range(COLS):
        for j in range(i + 1):
            a[i, j] = jnp.broadcast_to(entry_ref[pl.ds(i * (i + 1) // 2 + j, 1), :], (8, 128))
    low = {}
    for k in range(COLS):
        inverse = 1.0 / a[k, k]
        for i in range(k + 1, COLS):
            low[i, k] = a[i, k] * inverse
        for i in range(k + 1, COLS):
            for j in range(k + 1, i + 1):
                a[i, j] = a[i, j] - low[i, k] * a[j, k]
    lane = lax.broadcasted_iota(jnp.int32, (8, 128), 1) & 63
    rows = jnp.sqrt(jnp.float32(rows_total))
    shrink = 1.0 / jnp.sqrt(jnp.float32(rows_total * NFFT))
    turned = {}
    for i in range(COLS):
        scale = 1.0 / jnp.sqrt(a[i, i])
        left = jnp.where(lane == i, 1.0, 0.0)
        for j in range(i):
            x = low[i, j]
            for k in range(j + 1, i):
                x = x + low[i, k] * turned[k, j]
            turned[i, j] = -x
            left = jnp.where(lane == j, turned[i, j], left)
        left_ref[2 * i : 2 * i + 2, :] = (left * (scale * rows))[0:2]
        upper = jnp.zeros((8, 128), jnp.float32)
        for k in range(i, COLS):
            upper = jnp.where(lane == k, a[k, i], upper)
        upper = upper * (scale * shrink)
        triangle_ref[i] = jnp.where(
            lax.broadcasted_iota(jnp.int32, (8, 128), 0) == 0, upper, pltpu.roll(upper, 64, 1)
        )[0:2, 0:COLS]
    lane = lax.broadcasted_iota(jnp.int32, (32, 128), 1)
    row = lax.broadcasted_iota(jnp.int32, (32, 128), 0)
    left = left_ref[...]
    left = jnp.where((row & 1) == 0, jnp.where(lane < 16, left, 0.0), jnp.where((lane >= 16) & (lane < 32), pltpu.roll(left, 80, 1), 0.0))
    left = jnp.where(row < 2 * COLS, left, 0.0)
    left = left + pltpu.roll(left, 32, 1) + pltpu.roll(left, 64, 1)
    left = jnp.concatenate([x[:, 0:96] for x in pieces(left)], axis=0)
    copies = []
    for v in range(nvar):
        x = dot(left, stack_ref[:, v * cells : (v + 1) * cells])
        x = x[64:96] + x[32:64] + x[0:32]
        for j in range(COLS):
            modes_ref[j, v] = x[2 * j : 2 * j + 2, :]
        copies.append(pltpu.make_async_copy(modes_ref.at[:, v], modes_hbm.at[:, v], sem.at[v]))
        copies[-1].start()
    for copy in copies:
        copy.wait()


def modes_of(shares, stack, nvar, cells, cell_count):
    return pl.pallas_call(
        functools.partial(modes_kernel, nvar * cells * cell_count),
        out_shape=(
            jax.ShapeDtypeStruct((COLS, nvar, 2, cells), jnp.float32),
            jax.ShapeDtypeStruct((COLS, 2, COLS), jnp.float32),
        ),
        out_specs=(pl.BlockSpec(memory_space=pl.ANY), pl.BlockSpec(memory_space=pltpu.VMEM)),
        scratch_shapes=[
            pltpu.VMEM((COLS, nvar, 2, cells), jnp.float32),
            pltpu.VMEM((64, 128), jnp.float32),
            pltpu.VMEM((32, 128), jnp.float32),
            pltpu.SemaphoreType.DMA((nvar,)),
        ],
        compiler_params=pltpu.CompilerParams(vmem_limit_bytes=12 << 20),
        name="modes",
    )(shares, stack)


def chain(snapshots, volumes, freq_index, block_start, exchange, share, cell_count):
    tdev, nvar, cells = snapshots.shape
    parts = exchange(transform(snapshots, freq_index, block_start))
    stack, packed = gram(parts, volumes, cell_count)
    modes, triangle = modes_of(share(packed), stack, nvar, cells, cell_count)
    return jnp.transpose(modes, (2, 0, 1, 3)), jnp.transpose(triangle, (1, 0, 2))


def on_device(snapshots, volumes, freq_index, block_start):
    return chain(
        snapshots,
        volumes,
        freq_index,
        block_start,
        lambda x: lax.all_to_all(x, "tm", 0, 0, tiled=True),
        lambda x: lax.all_to_all(x, "cell", 0, 0, tiled=True),
        lax.axis_size("cell"),
    )


def solution(mesh):
    placed = (P("tm", None, "cell"), P("cell"), P(), P())
    return jax.shard_map(
        on_device,
        mesh=mesh,
        in_specs=placed,
        out_specs=(P("tm", None, None, "cell"), P("tm", None, None)),
        check_vma=False,
    )
```

```python
import functools

import jax
import jax.numpy as jnp
from jax import lax
from jax.experimental import pallas as pl
from jax.experimental.pallas import tpu as pltpu
from jax.sharding import PartitionSpec as P

NFFT = 128
NF = 8
NB = 5
COLS = 2 * NB
SLOTS = NB - 1
TWO_PI = 6.283185307179586


def pieces(x):
    high = x.astype(jnp.bfloat16)
    rest = x - high.astype(jnp.float32)
    middle = rest.astype(jnp.bfloat16)
    low = (rest - middle.astype(jnp.float32)).astype(jnp.bfloat16)
    return high, middle, low


def dot(a, b, contract=((1,), (0,))):
    return lax.dot_general(a, b, (contract, ((), ())), preferred_element_type=jnp.float32)


def transform_kernel(
    freq_hbm, start_hbm, vol_hbm, x_hbm, out_ref, freq_ref, start_ref, vol_ref, x_ref, table_ref, small_sem, in_sem
):
    nvar, tdev, cells = x_hbm.shape
    small = [
        pltpu.make_async_copy(freq_hbm, freq_ref, small_sem.at[0]),
        pltpu.make_async_copy(start_hbm, start_ref, small_sem.at[1]),
        pltpu.make_async_copy(vol_hbm, vol_ref, small_sem.at[2]),
    ]
    for copy in small:
        copy.start()
    for v in range(nvar):
        pltpu.make_async_copy(x_hbm.at[v], x_ref.at[v], in_sem.at[v]).start()
    quarter = lax.axis_index("tm")
    first = jnp.where(quarter >= 2, 1, 0)
    sub = lax.broadcasted_iota(jnp.int32, (8, tdev), 0)
    time = lax.broadcasted_iota(jnp.int32, (8, tdev), 1) + quarter * tdev
    slot = sub % SLOTS
    for copy in small:
        copy.wait()
    start = jnp.zeros((8, tdev), jnp.int32)
    for s in range(SLOTS):
        start = jnp.where(slot == s, start_ref[first + s], start)
    tau = time - start
    valid = (tau >= 0) & (tau < NFFT)
    hann = jnp.where(valid, 0.5 - 0.5 * jnp.cos(TWO_PI / NFFT * tau.astype(jnp.float32)), 0.0)
    turn = jnp.where(sub >= SLOTS, NFFT // 4, 0)
    rows = []
    for g in range(NF):
        phase = (freq_ref[g] * tau + turn) & (NFFT - 1)
        rows.append(hann * jnp.cos(TWO_PI / NFFT * phase.astype(jnp.float32)))
    high, middle, low = pieces(jnp.concatenate(rows, axis=0))
    table_ref[:, 0:tdev] = jnp.concatenate([high, middle, low], axis=0)
    table_ref[:, tdev : 2 * tdev] = jnp.concatenate([high, middle, jnp.zeros_like(low)], axis=0)
    root = jnp.sqrt(vol_ref[...]).reshape(1, cells)
    for v in range(nvar):
        at = slice(v * cells, (v + 1) * cells)
        pltpu.make_async_copy(x_hbm.at[v], x_ref.at[v], in_sem.at[v]).wait()
        x0, x1, x2 = pieces(x_ref[v])
        last = dot(table_ref[0:64, 0:tdev], x2)
        total = dot(table_ref[...], jnp.concatenate([x0, x1], axis=0))
        total = total[0:64] + (total[64:128] + (total[128:192] + last))
        out_ref[:, :, at] = (total * root).reshape(4, 16, cells)


def transform(snapshots, volumes, freq_index, block_start):
    tdev, nvar, cells = snapshots.shape
    x = jnp.transpose(snapshots, (1, 0, 2))
    return pl.pallas_call(
        transform_kernel,
        out_shape=jax.ShapeDtypeStruct((4, 16, nvar * cells), jnp.float32),
        in_specs=[pl.BlockSpec(memory_space=pltpu.HBM)] * 4,
        out_specs=pl.BlockSpec(memory_space=pltpu.VMEM),
        scratch_shapes=[
            pltpu.SMEM((NF,), jnp.int32),
            pltpu.SMEM((NB,), jnp.int32),
            pltpu.VMEM((cells,), jnp.float32),
            pltpu.VMEM((nvar, tdev, cells), jnp.float32),
            pltpu.VMEM((192, 2 * tdev), jnp.bfloat16),
            pltpu.SemaphoreType.DMA((3,)),
            pltpu.SemaphoreType.DMA((nvar,)),
        ],
        compiler_params=pltpu.CompilerParams(vmem_limit_bytes=8 << 20),
        name="transform",
    )(*(pltpu.with_memory_space_constraint(a, pltpu.HBM) for a in (freq_index, block_start, volumes, x)))


def gram_kernel(cells, parts_ref, stack_ref, packed_ref):
    sub = lax.broadcasted_iota(jnp.int32, (8, cells), 0)
    full = jnp.zeros((96, 96), jnp.float32)
    for v in range(parts_ref.shape[2] // cells):
        at = slice(v * cells, (v + 1) * cells)
        tiles = []
        for f in range(2):
            rows = slice(8 * f, 8 * f + 8)
            early = parts_ref[0, rows, at] + parts_ref[1, rows, at]
            late = parts_ref[2, rows, at] + parts_ref[3, rows, at]
            early1 = pltpu.roll(early, 1, 0)
            late1 = pltpu.roll(late, 1, 0)
            late2 = pltpu.roll(late, 2, 0)
            upper = jnp.where(sub < 4, early, jnp.where(sub >= 5, early1, 0.0))
            upper = upper + jnp.where((sub >= 1) & (sub < 5), late1, jnp.where(sub >= 6, late2, 0.0))
            lower = jnp.where(sub < 1, early1, 0.0) + jnp.where(sub < 2, late2, 0.0)
            tiles += [upper, lower]
        stack = jnp.concatenate(pieces(jnp.concatenate(tiles, axis=0)), axis=0)
        stack_ref[:, at] = stack
        full = full + dot(stack, stack, ((1,), (1,)))
    full = full[0:32] + full[32:64] + full[64:96]
    full = full[:, 0:32] + full[:, 32:64] + full[:, 64:96]
    full = jnp.concatenate([full, jnp.zeros((32, 96), jnp.float32)], axis=1)
    row = lax.broadcasted_iota(jnp.int32, (8, 128), 0)
    lane = lax.broadcasted_iota(jnp.int32, (8, 128), 1)
    moved = jnp.zeros((8, 128), jnp.float32)
    for f in range(2):
        for i in range(COLS):
            at = 16 * f + i // 8 * 8
            tile = jnp.where((row == i % 8) & (lane >= 16 * f) & (lane <= 16 * f + i), full[at : at + 8], 0.0)
            shift = 48 * f + i * (i + 1) // 2
            moved = moved + (pltpu.roll(tile, shift, 1) if shift else tile)
    packed_ref[...] = jnp.broadcast_to(jnp.sum(moved, axis=0, keepdims=True), packed_ref.shape)


def gram(parts, cells, cell_count):
    width = parts.shape[2]
    return pl.pallas_call(
        functools.partial(gram_kernel, cells),
        out_shape=(
            jax.ShapeDtypeStruct((96, width), jnp.bfloat16),
            jax.ShapeDtypeStruct((cell_count, 128), jnp.float32),
        ),
        compiler_params=pltpu.CompilerParams(vmem_limit_bytes=12 << 20),
        name="gram",
    )(parts)


def modes_kernel(rows_total, gram_ref, stack_ref, modes_hbm, triangle_ref, modes_ref, entry_ref, left_ref, sem):
    nvar = modes_ref.shape[1]
    cells = modes_ref.shape[3]
    total = jnp.broadcast_to(jnp.sum(gram_ref[...], axis=0, keepdims=True), (128, 128))
    total = jnp.transpose(total)
    entry_ref[...] = jnp.where(lax.broadcasted_iota(jnp.int32, (64, 128), 1) < 64, total[0:64], total[64:128])
    a = {}
    for i in range(COLS):
        for j in range(i + 1):
            a[i, j] = jnp.broadcast_to(entry_ref[pl.ds(i * (i + 1) // 2 + j, 1), :], (8, 128))
    low = {}
    for k in range(COLS):
        inverse = 1.0 / a[k, k]
        for i in range(k + 1, COLS):
            low[i, k] = a[i, k] * inverse
        for i in range(k + 1, COLS):
            for j in range(k + 1, i + 1):
                a[i, j] = a[i, j] - low[i, k] * a[j, k]
    lane = lax.broadcasted_iota(jnp.int32, (8, 128), 1) & 63
    rows = jnp.sqrt(jnp.float32(rows_total))
    shrink = 1.0 / jnp.sqrt(jnp.float32(rows_total * NFFT))
    turned = {}
    for i in range(COLS):
        scale = 1.0 / jnp.sqrt(a[i, i])
        left = jnp.where(lane == i, 1.0, 0.0)
        for j in range(i):
            x = low[i, j]
            for k in range(j + 1, i):
                x = x + low[i, k] * turned[k, j]
            turned[i, j] = -x
            left = jnp.where(lane == j, turned[i, j], left)
        left_ref[2 * i : 2 * i + 2, :] = (left * (scale * rows))[0:2]
        upper = jnp.zeros((8, 128), jnp.float32)
        for k in range(i, COLS):
            upper = jnp.where(lane == k, a[k, i], upper)
        upper = upper * (scale * shrink)
        triangle_ref[i] = jnp.where(
            lax.broadcasted_iota(jnp.int32, (8, 128), 0) == 0, upper, pltpu.roll(upper, 64, 1)
        )[0:2, 0:COLS]
    lane = lax.broadcasted_iota(jnp.int32, (32, 128), 1)
    row = lax.broadcasted_iota(jnp.int32, (32, 128), 0)
    left = left_ref[...]
    left = jnp.where((row & 1) == 0, jnp.where(lane < 16, left, 0.0), jnp.where((lane >= 16) & (lane < 32), pltpu.roll(left, 80, 1), 0.0))
    left = jnp.where(row < 2 * COLS, left, 0.0)
    left = left + pltpu.roll(left, 32, 1) + pltpu.roll(left, 64, 1)
    left = jnp.concatenate([x[:, 0:96] for x in pieces(left)], axis=0)
    copies = []
    for v in range(nvar):
        x = dot(left, stack_ref[:, v * cells : (v + 1) * cells])
        x = x[64:96] + x[32:64] + x[0:32]
        for j in range(COLS):
            modes_ref[j, v] = x[2 * j : 2 * j + 2, :]
        copies.append(pltpu.make_async_copy(modes_ref.at[:, v], modes_hbm.at[:, v], sem.at[v]))
        copies[-1].start()
    for copy in copies:
        copy.wait()


def modes_of(shares, stack, nvar, cells, cell_count):
    return pl.pallas_call(
        functools.partial(modes_kernel, nvar * cells * cell_count),
        out_shape=(
            jax.ShapeDtypeStruct((COLS, nvar, 2, cells), jnp.float32),
            jax.ShapeDtypeStruct((COLS, 2, COLS), jnp.float32),
        ),
        out_specs=(pl.BlockSpec(memory_space=pl.ANY), pl.BlockSpec(memory_space=pltpu.VMEM)),
        scratch_shapes=[
            pltpu.VMEM((COLS, nvar, 2, cells), jnp.float32),
            pltpu.VMEM((64, 128), jnp.float32),
            pltpu.VMEM((32, 128), jnp.float32),
            pltpu.SemaphoreType.DMA((nvar,)),
        ],
        compiler_params=pltpu.CompilerParams(vmem_limit_bytes=12 << 20),
        name="modes",
    )(shares, stack)


def chain(snapshots, volumes, freq_index, block_start, exchange, share, cell_count):
    tdev, nvar, cells = snapshots.shape
    parts = exchange(transform(snapshots, volumes, freq_index, block_start))
    stack, packed = gram(parts, cells, cell_count)
    modes, triangle = modes_of(share(packed), stack, nvar, cells, cell_count)
    return jnp.transpose(modes, (2, 0, 1, 3)), jnp.transpose(triangle, (1, 0, 2))


def on_device(snapshots, volumes, freq_index, block_start):
    return chain(
        snapshots,
        volumes,
        freq_index,
        block_start,
        lambda x: lax.all_to_all(x, "tm", 0, 0, tiled=True),
        lambda x: lax.all_to_all(x, "cell", 0, 0, tiled=True),
        lax.axis_size("cell"),
    )


def solution(mesh):
    placed = (P("tm", None, "cell"), P("cell"), P(), P())
    return jax.shard_map(
        on_device,
        mesh=mesh,
        in_specs=placed,
        out_specs=(P("tm", None, None, "cell"), P("tm", None, None)),
        check_vma=False,
    )
```

```python
import functools

import jax
import jax.numpy as jnp
from jax import lax
from jax.experimental import pallas as pl
from jax.experimental.pallas import tpu as pltpu
from jax.sharding import PartitionSpec as P

NFFT = 128
NF = 8
NB = 5
COLS = 2 * NB
SLOTS = NB - 1
TWO_PI = 6.283185307179586


def pieces(x):
    high = x.astype(jnp.bfloat16)
    rest = x - high.astype(jnp.float32)
    middle = rest.astype(jnp.bfloat16)
    low = (rest - middle.astype(jnp.float32)).astype(jnp.bfloat16)
    return high, middle, low


def dot(a, b, contract=((1,), (0,))):
    return lax.dot_general(a, b, (contract, ((), ())), preferred_element_type=jnp.float32)


def transform_kernel(
    freq_hbm, start_hbm, vol_hbm, x_hbm, out_ref, freq_ref, start_ref, vol_ref, x_ref, piece_ref, table_ref, small_sem, in_sem
):
    nvar, tdev, cells = x_hbm.shape

    def incoming(v):
        return pltpu.make_async_copy(x_hbm.at[v], x_ref.at[v], in_sem.at[v])

    small = [
        pltpu.make_async_copy(freq_hbm, freq_ref, small_sem.at[0]),
        pltpu.make_async_copy(start_hbm, start_ref, small_sem.at[1]),
        pltpu.make_async_copy(vol_hbm, vol_ref, small_sem.at[2]),
    ]
    for copy in small:
        copy.start()
    for v in range(nvar):
        incoming(v).start()
    quarter = lax.axis_index("tm")
    first = jnp.where(quarter >= 2, 1, 0)
    sub = lax.broadcasted_iota(jnp.int32, (8, tdev), 0)
    time = lax.broadcasted_iota(jnp.int32, (8, tdev), 1) + quarter * tdev
    slot = sub % SLOTS
    for copy in small:
        copy.wait()
    start = jnp.zeros((8, tdev), jnp.int32)
    for s in range(SLOTS):
        start = jnp.where(slot == s, start_ref[first + s], start)
    tau = time - start
    valid = (tau >= 0) & (tau < NFFT)
    hann = jnp.where(valid, 0.5 - 0.5 * jnp.cos(TWO_PI / NFFT * tau.astype(jnp.float32)), 0.0)
    turn = jnp.where(sub >= SLOTS, NFFT // 4, 0)
    rows = []
    for g in range(NF):
        phase = (freq_ref[g] * tau + turn) & (NFFT - 1)
        rows.append(hann * jnp.cos(TWO_PI / NFFT * phase.astype(jnp.float32)))
    high, middle, low = pieces(jnp.concatenate(rows, axis=0))
    table_ref[:, 0:tdev] = jnp.concatenate([high, middle, low], axis=0)
    table_ref[:, tdev : 2 * tdev] = jnp.concatenate([high, middle, high], axis=0)
    root = jnp.sqrt(vol_ref[...]).reshape(1, cells)

    def split(v, low):
        rows = slice(low, low + 16)
        x0, x1, x2 = pieces(x_ref[v, rows, :])
        piece_ref[v, low : low + 16, :] = x1
        piece_ref[v, tdev + low : tdev + low + 16, :] = x0
        piece_ref[v, 2 * tdev + low : 2 * tdev + low + 16, :] = x2

    def products(v, low):
        lanes = slice(low, low + 256)
        part = dot(table_ref[128:192], piece_ref[v, tdev : 3 * tdev, lanes])
        total = dot(table_ref[0:128], piece_ref[v, 0 : 2 * tdev, lanes])
        total = (total[0:64] + (total[64:128] + part)) * root[:, lanes]
        out_ref[:, :, v * cells + low : v * cells + low + 256] = total.reshape(4, 16, 256)

    blocks = tdev // 16
    tiles = cells // 256
    for v in range(nvar + 1):
        if v < nvar:
            incoming(v).wait()
        for n in range(tiles):
            if v < nvar:
                for r in range(n * blocks // tiles, (n + 1) * blocks // tiles):
                    split(v, 16 * r)
            if v > 0:
                products(v - 1, 256 * n)


def transform(snapshots, volumes, freq_index, block_start):
    tdev, nvar, cells = snapshots.shape
    x = jnp.transpose(snapshots, (1, 0, 2))
    return pl.pallas_call(
        transform_kernel,
        out_shape=jax.ShapeDtypeStruct((4, 16, nvar * cells), jnp.float32),
        in_specs=[pl.BlockSpec(memory_space=pltpu.HBM)] * 4,
        out_specs=pl.BlockSpec(memory_space=pltpu.VMEM),
        scratch_shapes=[
            pltpu.SMEM((NF,), jnp.int32),
            pltpu.SMEM((NB,), jnp.int32),
            pltpu.VMEM((cells,), jnp.float32),
            pltpu.VMEM((nvar, tdev, cells), jnp.float32),
            pltpu.VMEM((nvar, 3 * tdev, cells), jnp.bfloat16),
            pltpu.VMEM((192, 2 * tdev), jnp.bfloat16),
            pltpu.SemaphoreType.DMA((3,)),
            pltpu.SemaphoreType.DMA((nvar,)),
        ],
        compiler_params=pltpu.CompilerParams(vmem_limit_bytes=8 << 20),
        name="transform",
    )(*(pltpu.with_memory_space_constraint(a, pltpu.HBM) for a in (freq_index, block_start, volumes, x)))


def gram_kernel(cells, parts_ref, stack_ref, packed_ref):
    sub = lax.broadcasted_iota(jnp.int32, (8, cells), 0)
    full = jnp.zeros((96, 96), jnp.float32)
    for v in range(parts_ref.shape[2] // cells):
        at = slice(v * cells, (v + 1) * cells)
        tiles = []
        for f in range(2):
            rows = slice(8 * f, 8 * f + 8)
            early = parts_ref[0, rows, at] + parts_ref[1, rows, at]
            late = parts_ref[2, rows, at] + parts_ref[3, rows, at]
            early1 = pltpu.roll(early, 1, 0)
            late1 = pltpu.roll(late, 1, 0)
            late2 = pltpu.roll(late, 2, 0)
            upper = jnp.where(sub < 4, early, jnp.where(sub >= 5, early1, 0.0))
            upper = upper + jnp.where((sub >= 1) & (sub < 5), late1, jnp.where(sub >= 6, late2, 0.0))
            lower = jnp.where(sub < 1, early1, 0.0) + jnp.where(sub < 2, late2, 0.0)
            tiles += [upper, lower]
        stack = jnp.concatenate(pieces(jnp.concatenate(tiles, axis=0)), axis=0)
        stack_ref[:, at] = stack
        full = full + dot(stack, stack, ((1,), (1,)))
    full = full[0:32] + full[32:64] + full[64:96]
    full = full[:, 0:32] + full[:, 32:64] + full[:, 64:96]
    full = jnp.concatenate([full, jnp.zeros((32, 96), jnp.float32)], axis=1)
    row = lax.broadcasted_iota(jnp.int32, (8, 128), 0)
    lane = lax.broadcasted_iota(jnp.int32, (8, 128), 1)
    moved = jnp.zeros((8, 128), jnp.float32)
    for f in range(2):
        for i in range(COLS):
            at = 16 * f + i // 8 * 8
            tile = jnp.where((row == i % 8) & (lane >= 16 * f) & (lane <= 16 * f + i), full[at : at + 8], 0.0)
            shift = 48 * f + i * (i + 1) // 2
            moved = moved + (pltpu.roll(tile, shift, 1) if shift else tile)
    packed_ref[...] = jnp.broadcast_to(jnp.sum(moved, axis=0, keepdims=True), packed_ref.shape)


def gram(parts, cells, cell_count):
    width = parts.shape[2]
    return pl.pallas_call(
        functools.partial(gram_kernel, cells),
        out_shape=(
            jax.ShapeDtypeStruct((96, width), jnp.bfloat16),
            jax.ShapeDtypeStruct((cell_count, 128), jnp.float32),
        ),
        compiler_params=pltpu.CompilerParams(vmem_limit_bytes=12 << 20),
        name="gram",
    )(parts)


def modes_kernel(rows_total, gram_ref, stack_ref, modes_hbm, triangle_hbm, modes_ref, triangle_ref, entry_ref, left_ref, sem):
    nvar = modes_ref.shape[1]
    cells = modes_ref.shape[3]
    total = jnp.broadcast_to(jnp.sum(gram_ref[...], axis=0, keepdims=True), (128, 128))
    total = jnp.transpose(total)
    entry_ref[...] = jnp.where(lax.broadcasted_iota(jnp.int32, (64, 128), 1) < 64, total[0:64], total[64:128])
    a = {}
    for i in range(COLS):
        for j in range(i + 1):
            a[i, j] = jnp.broadcast_to(entry_ref[pl.ds(i * (i + 1) // 2 + j, 1), :], (8, 128))
    low = {}
    for k in range(COLS):
        inverse = 1.0 / a[k, k]
        for i in range(k + 1, COLS):
            low[i, k] = a[i, k] * inverse
        for i in range(k + 1, COLS):
            for j in range(k + 1, i + 1):
                a[i, j] = a[i, j] - low[i, k] * a[j, k]
    lane = lax.broadcasted_iota(jnp.int32, (8, 128), 1) & 63
    rows = jnp.sqrt(jnp.float32(rows_total))
    shrink = 1.0 / jnp.sqrt(jnp.float32(rows_total * NFFT))
    turned = {}
    for i in range(COLS):
        scale = 1.0 / jnp.sqrt(a[i, i])
        left = jnp.where(lane == i, 1.0, 0.0)
        for j in range(i):
            x = low[i, j]
            for k in range(j + 1, i):
                x = x + low[i, k] * turned[k, j]
            turned[i, j] = -x
            left = jnp.where(lane == j, turned[i, j], left)
        left_ref[2 * i : 2 * i + 2, :] = (left * (scale * rows))[0:2]
        upper = jnp.zeros((8, 128), jnp.float32)
        for k in range(i, COLS):
            upper = jnp.where(lane == k, a[k, i], upper)
        upper = upper * (scale * shrink)
        triangle_ref[i] = jnp.where(
            lax.broadcasted_iota(jnp.int32, (8, 128), 0) == 0, upper, pltpu.roll(upper, 64, 1)
        )[0:2, 0:COLS]
    lane = lax.broadcasted_iota(jnp.int32, (32, 128), 1)
    row = lax.broadcasted_iota(jnp.int32, (32, 128), 0)
    left = left_ref[...]
    left = jnp.where((row & 1) == 0, jnp.where(lane < 16, left, 0.0), jnp.where((lane >= 16) & (lane < 32), pltpu.roll(left, 80, 1), 0.0))
    left = jnp.where(row < 2 * COLS, left, 0.0)
    left = left + pltpu.roll(left, 32, 1) + pltpu.roll(left, 64, 1)
    left = jnp.concatenate([x[:, 0:96] for x in pieces(left)], axis=0)
    copies = [pltpu.make_async_copy(triangle_ref, triangle_hbm, sem.at[nvar])]
    copies[0].start()
    for v in range(nvar):
        x = dot(left, stack_ref[:, v * cells : (v + 1) * cells])
        x = x[64:96] + x[32:64] + x[0:32]
        for j in range(COLS):
            modes_ref[j, v] = x[2 * j : 2 * j + 2, :]
        copies.append(pltpu.make_async_copy(modes_ref.at[:, v], modes_hbm.at[:, v], sem.at[v]))
        copies[-1].start()
    for copy in copies:
        copy.wait()


def modes_of(shares, stack, nvar, cells, cell_count):
    return pl.pallas_call(
        functools.partial(modes_kernel, nvar * cells * cell_count),
        out_shape=(
            jax.ShapeDtypeStruct((COLS, nvar, 2, cells), jnp.float32),
            jax.ShapeDtypeStruct((COLS, 2, COLS), jnp.float32),
        ),
        out_specs=(pl.BlockSpec(memory_space=pltpu.HBM), pl.BlockSpec(memory_space=pltpu.HBM)),
        scratch_shapes=[
            pltpu.VMEM((COLS, nvar, 2, cells), jnp.float32),
            pltpu.VMEM((COLS, 2, COLS), jnp.float32),
            pltpu.VMEM((64, 128), jnp.float32),
            pltpu.VMEM((32, 128), jnp.float32),
            pltpu.SemaphoreType.DMA((nvar + 1,)),
        ],
        compiler_params=pltpu.CompilerParams(vmem_limit_bytes=12 << 20),
        name="modes",
    )(shares, stack)


def chain(snapshots, volumes, freq_index, block_start, exchange, share, cell_count):
    tdev, nvar, cells = snapshots.shape
    parts = exchange(transform(snapshots, volumes, freq_index, block_start))
    stack, packed = gram(parts, cells, cell_count)
    modes, triangle = modes_of(share(packed), stack, nvar, cells, cell_count)
    return jnp.transpose(modes, (2, 0, 1, 3)), jnp.transpose(triangle, (1, 0, 2))


def on_device(snapshots, volumes, freq_index, block_start):
    return chain(
        snapshots,
        volumes,
        freq_index,
        block_start,
        lambda x: lax.all_to_all(x, "tm", 0, 0, tiled=True),
        lambda x: lax.all_to_all(x, "cell", 0, 0, tiled=True),
        lax.axis_size("cell"),
    )


def solution(mesh):
    placed = (P("tm", None, "cell"), P("cell"), P(), P())
    return jax.shard_map(
        on_device,
        mesh=mesh,
        in_specs=placed,
        out_specs=(P("tm", None, None, "cell"), P("tm", None, None)),
        check_vma=False,
    )
```

```python
import functools

import jax
import jax.numpy as jnp
from jax import lax
from jax.experimental import pallas as pl
from jax.experimental.pallas import tpu as pltpu
from jax.sharding import PartitionSpec as P

NFFT = 128
NF = 8
NB = 5
COLS = 2 * NB
SLOTS = NB - 1
TWO_PI = 6.283185307179586
TM_ORDER = (2, 3, 0, 1)
CELL_FIRST = 72


def pieces(x):
    high = x.astype(jnp.bfloat16)
    rest = x - high.astype(jnp.float32)
    middle = rest.astype(jnp.bfloat16)
    low = (rest - middle.astype(jnp.float32)).astype(jnp.bfloat16)
    return high, middle, low


def dot(a, b, contract=((1,), (0,))):
    return lax.dot_general(a, b, (contract, ((), ())), preferred_element_type=jnp.float32)


def transform_kernel(
    freq_hbm, start_hbm, vol_hbm, x_hbm, out_ref, freq_ref, start_ref, vol_ref, x_ref, piece_ref, table_ref, small_sem, in_sem
):
    nvar, tdev, cells = x_hbm.shape

    def incoming(v):
        return pltpu.make_async_copy(x_hbm.at[v], x_ref.at[v], in_sem.at[v])

    small = [
        pltpu.make_async_copy(freq_hbm, freq_ref, small_sem.at[0]),
        pltpu.make_async_copy(start_hbm, start_ref, small_sem.at[1]),
        pltpu.make_async_copy(vol_hbm, vol_ref, small_sem.at[2]),
    ]
    for copy in small:
        copy.start()
    for v in range(nvar):
        incoming(v).start()
    quarter = lax.axis_index("tm")
    first = jnp.where(quarter >= 2, 1, 0)
    sub = lax.broadcasted_iota(jnp.int32, (8, tdev), 0)
    time = lax.broadcasted_iota(jnp.int32, (8, tdev), 1) + quarter * tdev
    slot = sub % SLOTS
    for copy in small:
        copy.wait()
    start = jnp.zeros((8, tdev), jnp.int32)
    for s in range(SLOTS):
        start = jnp.where(slot == s, start_ref[first + s], start)
    tau = time - start
    valid = (tau >= 0) & (tau < NFFT)
    hann = jnp.where(valid, 0.5 - 0.5 * jnp.cos(TWO_PI / NFFT * tau.astype(jnp.float32)), 0.0)
    turn = jnp.where(sub >= SLOTS, NFFT // 4, 0)
    rows = []
    for g in range(NF):
        phase = (freq_ref[2 * TM_ORDER[g // 2] + g % 2] * tau + turn) & (NFFT - 1)
        rows.append(hann * jnp.cos(TWO_PI / NFFT * phase.astype(jnp.float32)))
    high, middle, low = pieces(jnp.concatenate(rows, axis=0))
    table_ref[:, 0:tdev] = jnp.concatenate([high, middle, low], axis=0)
    table_ref[:, tdev : 2 * tdev] = jnp.concatenate([high, middle, high], axis=0)
    root = jnp.sqrt(vol_ref[...]).reshape(1, cells)

    def split(v, low):
        rows = slice(low, low + 16)
        x0, x1, x2 = pieces(x_ref[v, rows, :])
        piece_ref[v, low : low + 16, :] = x1
        piece_ref[v, tdev + low : tdev + low + 16, :] = x0
        piece_ref[v, 2 * tdev + low : 2 * tdev + low + 16, :] = x2

    def products(v, low):
        lanes = slice(low, low + 256)
        part = dot(table_ref[128:192], piece_ref[v, tdev : 3 * tdev, lanes])
        total = dot(table_ref[0:128], piece_ref[v, 0 : 2 * tdev, lanes])
        total = (total[0:64] + (total[64:128] + part)) * root[:, lanes]
        out_ref[:, :, v * cells + low : v * cells + low + 256] = total.reshape(4, 16, 256)

    blocks = tdev // 16
    tiles = cells // 256
    for v in range(nvar + 1):
        if v < nvar:
            incoming(v).wait()
        for n in range(tiles):
            if v < nvar:
                for r in range(n * blocks // tiles, (n + 1) * blocks // tiles):
                    split(v, 16 * r)
            if v > 0:
                products(v - 1, 256 * n)


def transform(snapshots, volumes, freq_index, block_start):
    tdev, nvar, cells = snapshots.shape
    x = jnp.transpose(snapshots, (1, 0, 2))
    return pl.pallas_call(
        transform_kernel,
        out_shape=jax.ShapeDtypeStruct((4, 16, nvar * cells), jnp.float32),
        in_specs=[pl.BlockSpec(memory_space=pltpu.HBM)] * 4,
        out_specs=pl.BlockSpec(memory_space=pltpu.VMEM),
        scratch_shapes=[
            pltpu.SMEM((NF,), jnp.int32),
            pltpu.SMEM((NB,), jnp.int32),
            pltpu.VMEM((cells,), jnp.float32),
            pltpu.VMEM((nvar, tdev, cells), jnp.float32),
            pltpu.VMEM((nvar, 3 * tdev, cells), jnp.bfloat16),
            pltpu.VMEM((192, 2 * tdev), jnp.bfloat16),
            pltpu.SemaphoreType.DMA((3,)),
            pltpu.SemaphoreType.DMA((nvar,)),
        ],
        compiler_params=pltpu.CompilerParams(vmem_limit_bytes=8 << 20),
        name="transform",
    )(*(pltpu.with_memory_space_constraint(a, pltpu.HBM) for a in (freq_index, block_start, volumes, x)))


def gram_kernel(cells, parts_ref, stack_ref, packed_ref):
    sub = lax.broadcasted_iota(jnp.int32, (8, cells), 0)
    full = jnp.zeros((96, 96), jnp.float32)
    place = [TM_ORDER.index(q) for q in range(4)]
    for v in range(parts_ref.shape[2] // cells):
        at = slice(v * cells, (v + 1) * cells)
        tiles = []
        for f in range(2):
            rows = slice(8 * f, 8 * f + 8)
            early = parts_ref[place[0], rows, at] + parts_ref[place[1], rows, at]
            late = parts_ref[place[2], rows, at] + parts_ref[place[3], rows, at]
            early1 = pltpu.roll(early, 1, 0)
            late1 = pltpu.roll(late, 1, 0)
            late2 = pltpu.roll(late, 2, 0)
            upper = jnp.where(sub < 4, early, jnp.where(sub >= 5, early1, 0.0))
            upper = upper + jnp.where((sub >= 1) & (sub < 5), late1, jnp.where(sub >= 6, late2, 0.0))
            lower = jnp.where(sub < 1, early1, 0.0) + jnp.where(sub < 2, late2, 0.0)
            tiles += [upper, lower]
        stack = jnp.concatenate(pieces(jnp.concatenate(tiles, axis=0)), axis=0)
        stack_ref[:, at] = stack
        full = full + dot(stack, stack, ((1,), (1,)))
    full = full[0:32] + full[32:64] + full[64:96]
    full = full[:, 0:32] + full[:, 32:64] + full[:, 64:96]
    full = jnp.concatenate([full, jnp.zeros((32, 96), jnp.float32)], axis=1)
    row = lax.broadcasted_iota(jnp.int32, (8, 128), 0)
    lane = lax.broadcasted_iota(jnp.int32, (8, 128), 1)
    moved = jnp.zeros((8, 128), jnp.float32)
    for f in range(2):
        for i in range(COLS):
            at = 16 * f + i // 8 * 8
            tile = jnp.where((row == i % 8) & (lane >= 16 * f) & (lane <= 16 * f + i), full[at : at + 8], 0.0)
            shift = 48 * f + i * (i + 1) // 2
            moved = moved + (pltpu.roll(tile, shift, 1) if shift else tile)
    packed_ref[...] = jnp.broadcast_to(jnp.sum(moved, axis=0, keepdims=True), packed_ref.shape)


def gram(parts, cells, cell_count):
    width = parts.shape[2]
    return pl.pallas_call(
        functools.partial(gram_kernel, cells),
        out_shape=(
            jax.ShapeDtypeStruct((96, width), jnp.bfloat16),
            jax.ShapeDtypeStruct((cell_count, 128), jnp.float32),
        ),
        compiler_params=pltpu.CompilerParams(vmem_limit_bytes=12 << 20),
        name="gram",
    )(parts)


def modes_kernel(rows_total, gram_ref, stack_ref, modes_hbm, triangle_hbm, modes_ref, triangle_ref, entry_ref, left_ref, sem):
    nvar = modes_ref.shape[1]
    cells = modes_ref.shape[3]
    total = jnp.broadcast_to(jnp.sum(gram_ref[...], axis=0, keepdims=True), (128, 128))
    total = jnp.transpose(total)
    entry_ref[...] = jnp.where(lax.broadcasted_iota(jnp.int32, (64, 128), 1) < 64, total[0:64], total[64:128])
    a = {}
    for i in range(COLS):
        for j in range(i + 1):
            a[i, j] = jnp.broadcast_to(entry_ref[pl.ds(i * (i + 1) // 2 + j, 1), :], (8, 128))
    low = {}
    for k in range(COLS):
        inverse = 1.0 / a[k, k]
        for i in range(k + 1, COLS):
            low[i, k] = a[i, k] * inverse
        for i in range(k + 1, COLS):
            for j in range(k + 1, i + 1):
                a[i, j] = a[i, j] - low[i, k] * a[j, k]
    lane = lax.broadcasted_iota(jnp.int32, (8, 128), 1) & 63
    rows = jnp.sqrt(jnp.float32(rows_total))
    shrink = 1.0 / jnp.sqrt(jnp.float32(rows_total * NFFT))
    turned = {}
    for i in range(COLS):
        scale = 1.0 / jnp.sqrt(a[i, i])
        left = jnp.where(lane == i, 1.0, 0.0)
        for j in range(i):
            x = low[i, j]
            for k in range(j + 1, i):
                x = x + low[i, k] * turned[k, j]
            turned[i, j] = -x
            left = jnp.where(lane == j, turned[i, j], left)
        left_ref[2 * i : 2 * i + 2, :] = (left * (scale * rows))[0:2]
        upper = jnp.zeros((8, 128), jnp.float32)
        for k in range(i, COLS):
            upper = jnp.where(lane == k, a[k, i], upper)
        upper = upper * (scale * shrink)
        triangle_ref[i] = jnp.where(
            lax.broadcasted_iota(jnp.int32, (8, 128), 0) == 0, upper, pltpu.roll(upper, 64, 1)
        )[0:2, 0:COLS]
    lane = lax.broadcasted_iota(jnp.int32, (32, 128), 1)
    row = lax.broadcasted_iota(jnp.int32, (32, 128), 0)
    left = left_ref[...]
    left = jnp.where((row & 1) == 0, jnp.where(lane < 16, left, 0.0), jnp.where((lane >= 16) & (lane < 32), pltpu.roll(left, 80, 1), 0.0))
    left = jnp.where(row < 2 * COLS, left, 0.0)
    left = left + pltpu.roll(left, 32, 1) + pltpu.roll(left, 64, 1)
    left = jnp.concatenate([x[:, 0:96] for x in pieces(left)], axis=0)
    copies = [pltpu.make_async_copy(triangle_ref, triangle_hbm, sem.at[nvar])]
    copies[0].start()
    for v in range(nvar):
        x = dot(left, stack_ref[:, v * cells : (v + 1) * cells])
        x = x[64:96] + x[32:64] + x[0:32]
        for j in range(COLS):
            modes_ref[j, v] = x[2 * j : 2 * j + 2, :]
        copies.append(pltpu.make_async_copy(modes_ref.at[:, v], modes_hbm.at[:, v], sem.at[v]))
        copies[-1].start()
    for copy in copies:
        copy.wait()


def modes_of(shares, stack, nvar, cells, cell_count):
    return pl.pallas_call(
        functools.partial(modes_kernel, nvar * cells * cell_count),
        out_shape=(
            jax.ShapeDtypeStruct((COLS, nvar, 2, cells), jnp.float32),
            jax.ShapeDtypeStruct((COLS, 2, COLS), jnp.float32),
        ),
        out_specs=(pl.BlockSpec(memory_space=pltpu.HBM), pl.BlockSpec(memory_space=pltpu.HBM)),
        scratch_shapes=[
            pltpu.VMEM((COLS, nvar, 2, cells), jnp.float32),
            pltpu.VMEM((COLS, 2, COLS), jnp.float32),
            pltpu.VMEM((64, 128), jnp.float32),
            pltpu.VMEM((32, 128), jnp.float32),
            pltpu.SemaphoreType.DMA((nvar + 1,)),
        ],
        compiler_params=pltpu.CompilerParams(vmem_limit_bytes=12 << 20),
        name="modes",
    )(shares, stack)


def chain(snapshots, volumes, freq_index, block_start, exchange, share, cell_count):
    tdev, nvar, cells = snapshots.shape
    parts = exchange(transform(snapshots, volumes, freq_index, block_start))
    stack, packed = gram(parts, cells, cell_count)
    modes, triangle = modes_of(share(packed), stack, nvar, cells, cell_count)
    return jnp.transpose(modes, (2, 0, 1, 3)), jnp.transpose(triangle, (1, 0, 2))


def cell_order(count):
    return [(CELL_FIRST + i) % count for i in range(count)]


def on_device(snapshots, volumes, freq_index, block_start):
    return chain(
        snapshots,
        volumes,
        freq_index,
        block_start,
        lambda x: lax.all_to_all(x, "tm", 0, 0, tiled=True, axis_index_groups=[list(TM_ORDER)]),
        lambda x: lax.all_to_all(x, "cell", 0, 0, tiled=True, axis_index_groups=[cell_order(lax.axis_size("cell"))]),
        lax.axis_size("cell"),
    )


def solution(mesh):
    placed = (P("tm", None, "cell"), P("cell"), P(), P())
    return jax.shard_map(
        on_device,
        mesh=mesh,
        in_specs=placed,
        out_specs=(P("tm", None, None, "cell"), P("tm", None, None)),
        check_vma=False,
    )
```

```python
import functools

import jax
import jax.numpy as jnp
from jax import lax
from jax.experimental import pallas as pl
from jax.experimental.pallas import tpu as pltpu
from jax.sharding import PartitionSpec as P

NFFT = 128
NF = 8
NB = 5
COLS = 2 * NB
SLOTS = NB - 1
TWO_PI = 6.283185307179586
TM_ORDER = (2, 0, 3, 1)
CELL_FIRST = 89


def pieces(x):
    high = x.astype(jnp.bfloat16)
    rest = x - high.astype(jnp.float32)
    middle = rest.astype(jnp.bfloat16)
    low = (rest - middle.astype(jnp.float32)).astype(jnp.bfloat16)
    return high, middle, low


def dot(a, b, contract=((1,), (0,))):
    return lax.dot_general(a, b, (contract, ((), ())), preferred_element_type=jnp.float32)


def transform_kernel(
    freq_hbm, start_hbm, vol_hbm, x_hbm, out_ref, freq_ref, start_ref, vol_ref, x_ref, piece_ref, table_ref, small_sem, in_sem
):
    nvar, tdev, cells = x_hbm.shape

    def incoming(v):
        return pltpu.make_async_copy(x_hbm.at[v], x_ref.at[v], in_sem.at[v])

    small = [
        pltpu.make_async_copy(freq_hbm, freq_ref, small_sem.at[0]),
        pltpu.make_async_copy(start_hbm, start_ref, small_sem.at[1]),
        pltpu.make_async_copy(vol_hbm, vol_ref, small_sem.at[2]),
    ]
    for copy in small:
        copy.start()
    for v in range(nvar):
        incoming(v).start()
    quarter = lax.axis_index("tm")
    first = jnp.where(quarter >= 2, 1, 0)
    sub = lax.broadcasted_iota(jnp.int32, (8, tdev), 0)
    time = lax.broadcasted_iota(jnp.int32, (8, tdev), 1) + quarter * tdev
    slot = sub % SLOTS
    for copy in small:
        copy.wait()
    start = jnp.zeros((8, tdev), jnp.int32)
    for s in range(SLOTS):
        start = jnp.where(slot == s, start_ref[first + s], start)
    tau = time - start
    valid = (tau >= 0) & (tau < NFFT)
    hann = jnp.where(valid, 0.5 - 0.5 * jnp.cos(TWO_PI / NFFT * tau.astype(jnp.float32)), 0.0)
    turn = jnp.where(sub >= SLOTS, NFFT // 4, 0)
    rows = []
    for g in range(NF):
        phase = (freq_ref[2 * TM_ORDER[g // 2] + g % 2] * tau + turn) & (NFFT - 1)
        rows.append(hann * jnp.cos(TWO_PI / NFFT * phase.astype(jnp.float32)))
    high, middle, low = pieces(jnp.concatenate(rows, axis=0))
    table_ref[:, 0:tdev] = jnp.concatenate([high, middle, low], axis=0)
    table_ref[:, tdev : 2 * tdev] = jnp.concatenate([high, middle, high], axis=0)
    root = jnp.sqrt(vol_ref[...]).reshape(1, cells)

    def split(v, low):
        rows = slice(low, low + 16)
        x0, x1, x2 = pieces(x_ref[v, rows, :])
        piece_ref[v, low : low + 16, :] = x1
        piece_ref[v, tdev + low : tdev + low + 16, :] = x0
        piece_ref[v, 2 * tdev + low : 2 * tdev + low + 16, :] = x2

    def products(v, low):
        lanes = slice(low, low + 256)
        part = dot(table_ref[128:192], piece_ref[v, tdev : 3 * tdev, lanes])
        total = dot(table_ref[0:128], piece_ref[v, 0 : 2 * tdev, lanes])
        total = (total[0:64] + (total[64:128] + part)) * root[:, lanes]
        out_ref[:, :, v * cells + low : v * cells + low + 256] = total.reshape(4, 16, 256)

    blocks = tdev // 16
    tiles = cells // 256
    for v in range(nvar + 1):
        if v < nvar:
            incoming(v).wait()
        for n in range(tiles):
            if v < nvar:
                for r in range(n * blocks // tiles, (n + 1) * blocks // tiles):
                    split(v, 16 * r)
            if v > 0:
                products(v - 1, 256 * n)


def transform(snapshots, volumes, freq_index, block_start):
    tdev, nvar, cells = snapshots.shape
    x = jnp.transpose(snapshots, (1, 0, 2))
    return pl.pallas_call(
        transform_kernel,
        out_shape=jax.ShapeDtypeStruct((4, 16, nvar * cells), jnp.float32),
        in_specs=[pl.BlockSpec(memory_space=pltpu.HBM)] * 4,
        out_specs=pl.BlockSpec(memory_space=pltpu.VMEM),
        scratch_shapes=[
            pltpu.SMEM((NF,), jnp.int32),
            pltpu.SMEM((NB,), jnp.int32),
            pltpu.VMEM((cells,), jnp.float32),
            pltpu.VMEM((nvar, tdev, cells), jnp.float32),
            pltpu.VMEM((nvar, 3 * tdev, cells), jnp.bfloat16),
            pltpu.VMEM((192, 2 * tdev), jnp.bfloat16),
            pltpu.SemaphoreType.DMA((3,)),
            pltpu.SemaphoreType.DMA((nvar,)),
        ],
        compiler_params=pltpu.CompilerParams(vmem_limit_bytes=8 << 20),
        name="transform",
    )(*(pltpu.with_memory_space_constraint(a, pltpu.HBM) for a in (freq_index, block_start, volumes, x)))


def gram_kernel(cells, parts_ref, stack_ref, packed_ref):
    sub = lax.broadcasted_iota(jnp.int32, (8, cells), 0)
    full = jnp.zeros((96, 96), jnp.float32)
    place = [TM_ORDER.index(q) for q in range(4)]
    for v in range(parts_ref.shape[2] // cells):
        at = slice(v * cells, (v + 1) * cells)
        tiles = []
        for f in range(2):
            rows = slice(8 * f, 8 * f + 8)
            early = parts_ref[place[0], rows, at] + parts_ref[place[1], rows, at]
            late = parts_ref[place[2], rows, at] + parts_ref[place[3], rows, at]
            early1 = pltpu.roll(early, 1, 0)
            late1 = pltpu.roll(late, 1, 0)
            late2 = pltpu.roll(late, 2, 0)
            upper = jnp.where(sub < 4, early, jnp.where(sub >= 5, early1, 0.0))
            upper = upper + jnp.where((sub >= 1) & (sub < 5), late1, jnp.where(sub >= 6, late2, 0.0))
            lower = jnp.where(sub < 1, early1, 0.0) + jnp.where(sub < 2, late2, 0.0)
            tiles += [upper, lower]
        stack = jnp.concatenate(pieces(jnp.concatenate(tiles, axis=0)), axis=0)
        stack_ref[:, at] = stack
        full = full + dot(stack, stack, ((1,), (1,)))
    full = full[0:32] + full[32:64] + full[64:96]
    full = full[:, 0:32] + full[:, 32:64] + full[:, 64:96]
    full = jnp.concatenate([full, jnp.zeros((32, 96), jnp.float32)], axis=1)
    row = lax.broadcasted_iota(jnp.int32, (8, 128), 0)
    lane = lax.broadcasted_iota(jnp.int32, (8, 128), 1)
    moved = jnp.zeros((8, 128), jnp.float32)
    for f in range(2):
        for i in range(COLS):
            at = 16 * f + i // 8 * 8
            tile = jnp.where((row == i % 8) & (lane >= 16 * f) & (lane <= 16 * f + i), full[at : at + 8], 0.0)
            shift = 48 * f + i * (i + 1) // 2
            moved = moved + (pltpu.roll(tile, shift, 1) if shift else tile)
    packed_ref[...] = jnp.broadcast_to(jnp.sum(moved, axis=0, keepdims=True), packed_ref.shape)


def gram(parts, cells, cell_count):
    width = parts.shape[2]
    return pl.pallas_call(
        functools.partial(gram_kernel, cells),
        out_shape=(
            jax.ShapeDtypeStruct((96, width), jnp.bfloat16),
            jax.ShapeDtypeStruct((cell_count, 128), jnp.float32),
        ),
        compiler_params=pltpu.CompilerParams(vmem_limit_bytes=12 << 20),
        name="gram",
    )(parts)


def modes_kernel(rows_total, gram_ref, stack_ref, modes_hbm, triangle_hbm, modes_ref, triangle_ref, entry_ref, left_ref, sem):
    nvar = modes_ref.shape[1]
    cells = modes_ref.shape[3]
    total = jnp.broadcast_to(jnp.sum(gram_ref[...], axis=0, keepdims=True), (128, 128))
    total = jnp.transpose(total)
    entry_ref[...] = jnp.where(lax.broadcasted_iota(jnp.int32, (64, 128), 1) < 64, total[0:64], total[64:128])
    a = {}
    for i in range(COLS):
        for j in range(i + 1):
            a[i, j] = jnp.broadcast_to(entry_ref[pl.ds(i * (i + 1) // 2 + j, 1), :], (8, 128))
    low = {}
    for k in range(COLS):
        inverse = 1.0 / a[k, k]
        for i in range(k + 1, COLS):
            low[i, k] = a[i, k] * inverse
        for i in range(k + 1, COLS):
            for j in range(k + 1, i + 1):
                a[i, j] = a[i, j] - low[i, k] * a[j, k]
    lane = lax.broadcasted_iota(jnp.int32, (8, 128), 1) & 63
    rows = jnp.sqrt(jnp.float32(rows_total))
    shrink = 1.0 / jnp.sqrt(jnp.float32(rows_total * NFFT))
    turned = {}
    for i in range(COLS):
        scale = 1.0 / jnp.sqrt(a[i, i])
        left = jnp.where(lane == i, 1.0, 0.0)
        for j in range(i):
            x = low[i, j]
            for k in range(j + 1, i):
                x = x + low[i, k] * turned[k, j]
            turned[i, j] = -x
            left = jnp.where(lane == j, turned[i, j], left)
        left_ref[2 * i : 2 * i + 2, :] = (left * (scale * rows))[0:2]
        upper = jnp.zeros((8, 128), jnp.float32)
        for k in range(i, COLS):
            upper = jnp.where(lane == k, a[k, i], upper)
        upper = upper * (scale * shrink)
        triangle_ref[i] = jnp.where(
            lax.broadcasted_iota(jnp.int32, (8, 128), 0) == 0, upper, pltpu.roll(upper, 64, 1)
        )[0:2, 0:COLS]
    lane = lax.broadcasted_iota(jnp.int32, (32, 128), 1)
    row = lax.broadcasted_iota(jnp.int32, (32, 128), 0)
    left = left_ref[...]
    left = jnp.where((row & 1) == 0, jnp.where(lane < 16, left, 0.0), jnp.where((lane >= 16) & (lane < 32), pltpu.roll(left, 80, 1), 0.0))
    left = jnp.where(row < 2 * COLS, left, 0.0)
    left = left + pltpu.roll(left, 32, 1) + pltpu.roll(left, 64, 1)
    left = jnp.concatenate([x[:, 0:96] for x in pieces(left)], axis=0)
    copies = [pltpu.make_async_copy(triangle_ref, triangle_hbm, sem.at[nvar])]
    copies[0].start()
    for v in range(nvar):
        x = dot(left, stack_ref[:, v * cells : (v + 1) * cells])
        x = x[64:96] + x[32:64] + x[0:32]
        for j in range(COLS):
            modes_ref[j, v] = x[2 * j : 2 * j + 2, :]
        copies.append(pltpu.make_async_copy(modes_ref.at[:, v], modes_hbm.at[:, v], sem.at[v]))
        copies[-1].start()
    for copy in copies:
        copy.wait()


def modes_of(shares, stack, nvar, cells, cell_count):
    return pl.pallas_call(
        functools.partial(modes_kernel, nvar * cells * cell_count),
        out_shape=(
            jax.ShapeDtypeStruct((COLS, nvar, 2, cells), jnp.float32),
            jax.ShapeDtypeStruct((COLS, 2, COLS), jnp.float32),
        ),
        out_specs=(pl.BlockSpec(memory_space=pltpu.HBM), pl.BlockSpec(memory_space=pltpu.HBM)),
        scratch_shapes=[
            pltpu.VMEM((COLS, nvar, 2, cells), jnp.float32),
            pltpu.VMEM((COLS, 2, COLS), jnp.float32),
            pltpu.VMEM((64, 128), jnp.float32),
            pltpu.VMEM((32, 128), jnp.float32),
            pltpu.SemaphoreType.DMA((nvar + 1,)),
        ],
        compiler_params=pltpu.CompilerParams(vmem_limit_bytes=12 << 20),
        name="modes",
    )(shares, stack)


def chain(snapshots, volumes, freq_index, block_start, exchange, share, cell_count):
    tdev, nvar, cells = snapshots.shape
    parts = exchange(transform(snapshots, volumes, freq_index, block_start))
    stack, packed = gram(parts, cells, cell_count)
    modes, triangle = modes_of(share(packed), stack, nvar, cells, cell_count)
    return jnp.transpose(modes, (2, 0, 1, 3)), jnp.transpose(triangle, (1, 0, 2))


def cell_order(count):
    return [(CELL_FIRST + i) % count for i in range(count)]


def on_device(snapshots, volumes, freq_index, block_start):
    return chain(
        snapshots,
        volumes,
        freq_index,
        block_start,
        lambda x: lax.all_to_all(x, "tm", 0, 0, tiled=True, axis_index_groups=[list(TM_ORDER)]),
        lambda x: lax.all_to_all(x, "cell", 0, 0, tiled=True, axis_index_groups=[cell_order(lax.axis_size("cell"))]),
        lax.axis_size("cell"),
    )


def solution(mesh):
    placed = (P("tm", None, "cell"), P("cell"), P(), P())
    return jax.shard_map(
        on_device,
        mesh=mesh,
        in_specs=placed,
        out_specs=(P("tm", None, None, "cell"), P("tm", None, None)),
        check_vma=False,
    )
```

```python
import functools

import jax
import jax.numpy as jnp
from jax import lax
from jax.experimental import pallas as pl
from jax.experimental.pallas import tpu as pltpu
from jax.sharding import PartitionSpec as P

NFFT = 128
NF = 8
NB = 5
COLS = 2 * NB
SLOTS = NB - 1
TWO_PI = 6.283185307179586
TM_ORDER = (2, 0, 3, 1)
CELL_FIRST = 89


def pieces(x):
    high = x.astype(jnp.bfloat16)
    rest = x - high.astype(jnp.float32)
    middle = rest.astype(jnp.bfloat16)
    low = (rest - middle.astype(jnp.float32)).astype(jnp.bfloat16)
    return high, middle, low


def dot(a, b, contract=((1,), (0,))):
    return lax.dot_general(a, b, (contract, ((), ())), preferred_element_type=jnp.float32)


def transform_kernel(
    freq_hbm, start_hbm, vol_hbm, x_hbm, out_ref, freq_ref, start_ref, vol_ref, x_ref, piece_ref, table_ref, small_sem, in_sem
):
    nvar, tdev, cells = x_hbm.shape

    def incoming(v):
        return pltpu.make_async_copy(x_hbm.at[v], x_ref.at[v], in_sem.at[v])

    small = [
        pltpu.make_async_copy(freq_hbm, freq_ref, small_sem.at[0]),
        pltpu.make_async_copy(start_hbm, start_ref, small_sem.at[1]),
        pltpu.make_async_copy(vol_hbm, vol_ref, small_sem.at[2]),
    ]
    for copy in small:
        copy.start()
    for v in range(nvar):
        incoming(v).start()
    quarter = lax.axis_index("tm")
    first = jnp.where(quarter >= 2, 1, 0)
    sub = lax.broadcasted_iota(jnp.int32, (8, NFFT), 0)
    lane = lax.broadcasted_iota(jnp.int32, (8, NFFT), 1)
    time = lane + quarter * tdev
    turns = jnp.cos(TWO_PI / NFFT * lane.astype(jnp.float32))
    slot = sub % SLOTS
    for copy in small:
        copy.wait()
    start = jnp.zeros((8, NFFT), jnp.int32)
    for s in range(SLOTS):
        start = jnp.where(slot == s, start_ref[first + s], start)
    tau = time - start
    valid = (tau >= 0) & (tau < NFFT)
    hann = jnp.where(valid, 0.5 - 0.5 * jnp.take_along_axis(turns, tau & (NFFT - 1), axis=1), 0.0)
    turn = jnp.where(sub >= SLOTS, NFFT // 4, 0)
    rows = []
    for g in range(NF):
        phase = (freq_ref[2 * TM_ORDER[g // 2] + g % 2] * tau + turn) & (NFFT - 1)
        rows.append((hann * jnp.take_along_axis(turns, phase, axis=1))[:, 0:tdev])
    high, middle, low = pieces(jnp.concatenate(rows, axis=0))
    table_ref[:, 0:tdev] = jnp.concatenate([high, middle, low], axis=0)
    table_ref[:, tdev : 2 * tdev] = jnp.concatenate([high, middle, high], axis=0)
    root = jnp.sqrt(vol_ref[...]).reshape(1, cells)

    def split(v, low):
        rows = slice(low, low + 16)
        x0, x1, x2 = pieces(x_ref[v, rows, :])
        piece_ref[v, low : low + 16, :] = x1
        piece_ref[v, tdev + low : tdev + low + 16, :] = x0
        piece_ref[v, 2 * tdev + low : 2 * tdev + low + 16, :] = x2

    def products(v, low):
        lanes = slice(low, low + 256)
        part = dot(table_ref[128:192], piece_ref[v, tdev : 3 * tdev, lanes])
        total = dot(table_ref[0:128], piece_ref[v, 0 : 2 * tdev, lanes])
        total = (total[0:64] + (total[64:128] + part)) * root[:, lanes]
        out_ref[:, :, v * cells + low : v * cells + low + 256] = total.reshape(4, 16, 256)

    for v in range(nvar):
        incoming(v).wait()
        for low in range(0, tdev, 16):
            split(v, low)
    for low in range(0, cells, 256):
        for v in range(nvar):
            products(v, low)


def transform(snapshots, volumes, freq_index, block_start):
    tdev, nvar, cells = snapshots.shape
    x = jnp.transpose(snapshots, (1, 0, 2))
    return pl.pallas_call(
        transform_kernel,
        out_shape=jax.ShapeDtypeStruct((4, 16, nvar * cells), jnp.float32),
        in_specs=[pl.BlockSpec(memory_space=pltpu.HBM)] * 4,
        out_specs=pl.BlockSpec(memory_space=pltpu.VMEM),
        scratch_shapes=[
            pltpu.SMEM((NF,), jnp.int32),
            pltpu.SMEM((NB,), jnp.int32),
            pltpu.VMEM((cells,), jnp.float32),
            pltpu.VMEM((nvar, tdev, cells), jnp.float32),
            pltpu.VMEM((nvar, 3 * tdev, cells), jnp.bfloat16),
            pltpu.VMEM((192, 2 * tdev), jnp.bfloat16),
            pltpu.SemaphoreType.DMA((3,)),
            pltpu.SemaphoreType.DMA((nvar,)),
        ],
        compiler_params=pltpu.CompilerParams(vmem_limit_bytes=8 << 20),
        name="transform",
    )(*(pltpu.with_memory_space_constraint(a, pltpu.HBM) for a in (freq_index, block_start, volumes, x)))


def gram_kernel(cells, parts_ref, stack_ref, packed_ref):
    sub = lax.broadcasted_iota(jnp.int32, (8, cells), 0)
    full = jnp.zeros((96, 96), jnp.float32)
    place = [TM_ORDER.index(q) for q in range(4)]
    for v in range(parts_ref.shape[2] // cells):
        at = slice(v * cells, (v + 1) * cells)
        tiles = []
        for f in range(2):
            rows = slice(8 * f, 8 * f + 8)
            early = parts_ref[place[0], rows, at] + parts_ref[place[1], rows, at]
            late = parts_ref[place[2], rows, at] + parts_ref[place[3], rows, at]
            early1 = pltpu.roll(early, 1, 0)
            late1 = pltpu.roll(late, 1, 0)
            late2 = pltpu.roll(late, 2, 0)
            upper = jnp.where(sub < 4, early, jnp.where(sub >= 5, early1, 0.0))
            upper = upper + jnp.where((sub >= 1) & (sub < 5), late1, jnp.where(sub >= 6, late2, 0.0))
            lower = jnp.where(sub < 1, early1, 0.0) + jnp.where(sub < 2, late2, 0.0)
            tiles += [upper, lower]
        stack = jnp.concatenate(pieces(jnp.concatenate(tiles, axis=0)), axis=0)
        stack_ref[:, at] = stack
        full = full + dot(stack, stack, ((1,), (1,)))
    full = full[0:32] + full[32:64] + full[64:96]
    full = full[:, 0:32] + full[:, 32:64] + full[:, 64:96]
    full = jnp.concatenate([full, jnp.zeros((32, 96), jnp.float32)], axis=1)
    row = lax.broadcasted_iota(jnp.int32, (8, 128), 0)
    lane = lax.broadcasted_iota(jnp.int32, (8, 128), 1)
    moved = jnp.zeros((8, 128), jnp.float32)
    for f in range(2):
        for i in range(COLS):
            at = 16 * f + i // 8 * 8
            tile = jnp.where((row == i % 8) & (lane >= 16 * f) & (lane <= 16 * f + i), full[at : at + 8], 0.0)
            shift = 48 * f + i * (i + 1) // 2
            moved = moved + (pltpu.roll(tile, shift, 1) if shift else tile)
    packed_ref[...] = jnp.broadcast_to(jnp.sum(moved, axis=0, keepdims=True), packed_ref.shape)


def gram(parts, cells, cell_count):
    width = parts.shape[2]
    return pl.pallas_call(
        functools.partial(gram_kernel, cells),
        out_shape=(
            jax.ShapeDtypeStruct((96, width), jnp.bfloat16),
            jax.ShapeDtypeStruct((cell_count, 128), jnp.float32),
        ),
        compiler_params=pltpu.CompilerParams(vmem_limit_bytes=12 << 20),
        name="gram",
    )(parts)


def modes_kernel(rows_total, gram_ref, stack_ref, modes_hbm, triangle_hbm, modes_ref, triangle_ref, entry_ref, left_ref, sem):
    nvar = modes_ref.shape[1]
    cells = modes_ref.shape[3]
    total = jnp.broadcast_to(jnp.sum(gram_ref[...], axis=0, keepdims=True), (128, 128))
    total = jnp.transpose(total)
    entry_ref[...] = jnp.where(lax.broadcasted_iota(jnp.int32, (64, 128), 1) < 64, total[0:64], total[64:128])
    a = {}
    for i in range(COLS):
        for j in range(i + 1):
            a[i, j] = jnp.broadcast_to(entry_ref[pl.ds(i * (i + 1) // 2 + j, 1), :], (8, 128))
    low = {}
    for k in range(COLS):
        inverse = 1.0 / a[k, k]
        for i in range(k + 1, COLS):
            low[i, k] = a[i, k] * inverse
        for i in range(k + 1, COLS):
            for j in range(k + 1, i + 1):
                a[i, j] = a[i, j] - low[i, k] * a[j, k]
    lane = lax.broadcasted_iota(jnp.int32, (8, 128), 1) & 63
    rows = jnp.sqrt(jnp.float32(rows_total))
    shrink = 1.0 / jnp.sqrt(jnp.float32(rows_total * NFFT))
    turned = {}
    for i in range(COLS):
        scale = 1.0 / jnp.sqrt(a[i, i])
        left = jnp.where(lane == i, 1.0, 0.0)
        for j in range(i):
            x = low[i, j]
            for k in range(j + 1, i):
                x = x + low[i, k] * turned[k, j]
            turned[i, j] = -x
            left = jnp.where(lane == j, turned[i, j], left)
        left_ref[2 * i : 2 * i + 2, :] = (left * (scale * rows))[0:2]
        upper = jnp.zeros((8, 128), jnp.float32)
        for k in range(i, COLS):
            upper = jnp.where(lane == k, a[k, i], upper)
        upper = upper * (scale * shrink)
        triangle_ref[i] = jnp.where(
            lax.broadcasted_iota(jnp.int32, (8, 128), 0) == 0, upper, pltpu.roll(upper, 64, 1)
        )[0:2, 0:COLS]
    lane = lax.broadcasted_iota(jnp.int32, (32, 128), 1)
    row = lax.broadcasted_iota(jnp.int32, (32, 128), 0)
    left = left_ref[...]
    left = jnp.where((row & 1) == 0, jnp.where(lane < 16, left, 0.0), jnp.where((lane >= 16) & (lane < 32), pltpu.roll(left, 80, 1), 0.0))
    left = jnp.where(row < 2 * COLS, left, 0.0)
    left = left + pltpu.roll(left, 32, 1) + pltpu.roll(left, 64, 1)
    left = jnp.concatenate([x[:, 0:96] for x in pieces(left)], axis=0)
    copies = [pltpu.make_async_copy(triangle_ref, triangle_hbm, sem.at[nvar])]
    copies[0].start()
    for v in range(nvar):
        x = dot(left, stack_ref[:, v * cells : (v + 1) * cells])
        x = x[64:96] + x[32:64] + x[0:32]
        for j in range(COLS):
            modes_ref[j, v] = x[2 * j : 2 * j + 2, :]
        copies.append(pltpu.make_async_copy(modes_ref.at[:, v], modes_hbm.at[:, v], sem.at[v]))
        copies[-1].start()
    for copy in copies:
        copy.wait()


def modes_of(shares, stack, nvar, cells, cell_count):
    return pl.pallas_call(
        functools.partial(modes_kernel, nvar * cells * cell_count),
        out_shape=(
            jax.ShapeDtypeStruct((COLS, nvar, 2, cells), jnp.float32),
            jax.ShapeDtypeStruct((COLS, 2, COLS), jnp.float32),
        ),
        out_specs=(pl.BlockSpec(memory_space=pltpu.HBM), pl.BlockSpec(memory_space=pltpu.HBM)),
        scratch_shapes=[
            pltpu.VMEM((COLS, nvar, 2, cells), jnp.float32),
            pltpu.VMEM((COLS, 2, COLS), jnp.float32),
            pltpu.VMEM((64, 128), jnp.float32),
            pltpu.VMEM((32, 128), jnp.float32),
            pltpu.SemaphoreType.DMA((nvar + 1,)),
        ],
        compiler_params=pltpu.CompilerParams(vmem_limit_bytes=12 << 20),
        name="modes",
    )(shares, stack)


def chain(snapshots, volumes, freq_index, block_start, exchange, share, cell_count):
    tdev, nvar, cells = snapshots.shape
    parts = exchange(transform(snapshots, volumes, freq_index, block_start))
    stack, packed = gram(parts, cells, cell_count)
    modes, triangle = modes_of(share(packed), stack, nvar, cells, cell_count)
    return jnp.transpose(modes, (2, 0, 1, 3)), jnp.transpose(triangle, (1, 0, 2))


def cell_order(count):
    return [(CELL_FIRST + i) % count for i in range(count)]


def on_device(snapshots, volumes, freq_index, block_start):
    return chain(
        snapshots,
        volumes,
        freq_index,
        block_start,
        lambda x: lax.all_to_all(x, "tm", 0, 0, tiled=True, axis_index_groups=[list(TM_ORDER)]),
        lambda x: lax.all_to_all(x, "cell", 0, 0, tiled=True, axis_index_groups=[cell_order(lax.axis_size("cell"))]),
        lax.axis_size("cell"),
    )


def solution(mesh):
    placed = (P("tm", None, "cell"), P("cell"), P(), P())
    return jax.shard_map(
        on_device,
        mesh=mesh,
        in_specs=placed,
        out_specs=(P("tm", None, None, "cell"), P("tm", None, None)),
        check_vma=False,
    )
```

```python
import functools

import jax
import jax.numpy as jnp
from jax import lax
from jax.experimental import pallas as pl
from jax.experimental.pallas import tpu as pltpu
from jax.sharding import PartitionSpec as P

NFFT = 128
NF = 8
NB = 5
COLS = 2 * NB
SLOTS = NB - 1
TWO_PI = 6.283185307179586
TM_ORDER = (2, 1, 3, 0)
CELL_FIRST = 105


def pieces(x):
    high = x.astype(jnp.bfloat16)
    rest = x - high.astype(jnp.float32)
    middle = rest.astype(jnp.bfloat16)
    low = (rest - middle.astype(jnp.float32)).astype(jnp.bfloat16)
    return high, middle, low


def dot(a, b, contract=((1,), (0,))):
    return lax.dot_general(a, b, (contract, ((), ())), preferred_element_type=jnp.float32)


def transform_kernel(
    freq_hbm, start_hbm, vol_hbm, x_hbm, out_ref, freq_ref, start_ref, vol_ref, x_ref, piece_ref, table_ref, small_sem, in_sem
):
    nvar, tdev, cells = x_hbm.shape

    def incoming(v):
        return pltpu.make_async_copy(x_hbm.at[v], x_ref.at[v], in_sem.at[v])

    small = [
        pltpu.make_async_copy(freq_hbm, freq_ref, small_sem.at[0]),
        pltpu.make_async_copy(start_hbm, start_ref, small_sem.at[1]),
        pltpu.make_async_copy(vol_hbm, vol_ref, small_sem.at[2]),
    ]
    for copy in small:
        copy.start()
    for v in range(nvar):
        incoming(v).start()
    quarter = lax.axis_index("tm")
    first = jnp.where(quarter >= 2, 1, 0)
    sub = lax.broadcasted_iota(jnp.int32, (8, NFFT), 0)
    lane = lax.broadcasted_iota(jnp.int32, (8, NFFT), 1)
    time = lane + quarter * tdev
    turns = jnp.cos(TWO_PI / NFFT * lane.astype(jnp.float32))
    slot = sub % SLOTS
    for copy in small:
        copy.wait()
    start = jnp.zeros((8, NFFT), jnp.int32)
    for s in range(SLOTS):
        start = jnp.where(slot == s, start_ref[first + s], start)
    tau = time - start
    valid = (tau >= 0) & (tau < NFFT)
    hann = jnp.where(valid, 0.5 - 0.5 * jnp.take_along_axis(turns, tau & (NFFT - 1), axis=1), 0.0)
    turn = jnp.where(sub >= SLOTS, NFFT // 4, 0)
    rows = []
    for g in range(NF):
        phase = (freq_ref[2 * TM_ORDER[g // 2] + g % 2] * tau + turn) & (NFFT - 1)
        rows.append((hann * jnp.take_along_axis(turns, phase, axis=1))[:, 0:tdev])
    high, middle, low = pieces(jnp.concatenate(rows, axis=0))
    table_ref[:, 0:tdev] = jnp.concatenate([high, middle, low], axis=0)
    table_ref[:, tdev : 2 * tdev] = jnp.concatenate([high, middle, high], axis=0)
    root = jnp.sqrt(vol_ref[...]).reshape(1, cells)

    def split(v, low):
        rows = slice(low, low + 16)
        x0, x1, x2 = pieces(x_ref[v, rows, :])
        piece_ref[v, low : low + 16, :] = x1
        piece_ref[v, tdev + low : tdev + low + 16, :] = x0
        piece_ref[v, 2 * tdev + low : 2 * tdev + low + 16, :] = x2

    def products(v, low):
        lanes = slice(low, low + 256)
        part = dot(table_ref[128:192], piece_ref[v, tdev : 3 * tdev, lanes])
        total = dot(table_ref[0:128], piece_ref[v, 0 : 2 * tdev, lanes])
        total = (total[0:64] + (total[64:128] + part)) * root[:, lanes]
        out_ref[:, :, v * cells + low : v * cells + low + 256] = total.reshape(4, 16, 256)

    for v in range(nvar):
        incoming(v).wait()
        for low in range(0, tdev, 16):
            split(v, low)
    for low in range(0, cells, 256):
        for v in range(nvar):
            products(v, low)


def transform(snapshots, volumes, freq_index, block_start):
    tdev, nvar, cells = snapshots.shape
    x = jnp.transpose(snapshots, (1, 0, 2))
    return pl.pallas_call(
        transform_kernel,
        out_shape=jax.ShapeDtypeStruct((4, 16, nvar * cells), jnp.float32),
        in_specs=[pl.BlockSpec(memory_space=pltpu.HBM)] * 4,
        out_specs=pl.BlockSpec(memory_space=pltpu.VMEM),
        scratch_shapes=[
            pltpu.SMEM((NF,), jnp.int32),
            pltpu.SMEM((NB,), jnp.int32),
            pltpu.VMEM((cells,), jnp.float32),
            pltpu.VMEM((nvar, tdev, cells), jnp.float32),
            pltpu.VMEM((nvar, 3 * tdev, cells), jnp.bfloat16),
            pltpu.VMEM((192, 2 * tdev), jnp.bfloat16),
            pltpu.SemaphoreType.DMA((3,)),
            pltpu.SemaphoreType.DMA((nvar,)),
        ],
        compiler_params=pltpu.CompilerParams(vmem_limit_bytes=8 << 20),
        name="transform",
    )(*(pltpu.with_memory_space_constraint(a, pltpu.HBM) for a in (freq_index, block_start, volumes, x)))


def gram_kernel(cells, parts_ref, stack_ref, packed_ref):
    sub = lax.broadcasted_iota(jnp.int32, (8, cells), 0)
    full = jnp.zeros((96, 96), jnp.float32)
    place = [TM_ORDER.index(q) for q in range(4)]
    for v in range(parts_ref.shape[2] // cells):
        at = slice(v * cells, (v + 1) * cells)
        tiles = []
        for f in range(2):
            rows = slice(8 * f, 8 * f + 8)
            early = parts_ref[place[0], rows, at] + parts_ref[place[1], rows, at]
            late = parts_ref[place[2], rows, at] + parts_ref[place[3], rows, at]
            early1 = pltpu.roll(early, 1, 0)
            late1 = pltpu.roll(late, 1, 0)
            late2 = pltpu.roll(late, 2, 0)
            upper = jnp.where(sub < 4, early, jnp.where(sub >= 5, early1, 0.0))
            upper = upper + jnp.where((sub >= 1) & (sub < 5), late1, jnp.where(sub >= 6, late2, 0.0))
            lower = jnp.where(sub < 1, early1, 0.0) + jnp.where(sub < 2, late2, 0.0)
            tiles += [upper, lower]
        stack = jnp.concatenate(pieces(jnp.concatenate(tiles, axis=0)), axis=0)
        stack_ref[:, at] = stack
        full = full + dot(stack, stack, ((1,), (1,)))
    full = full[0:32] + full[32:64] + full[64:96]
    full = full[:, 0:32] + full[:, 32:64] + full[:, 64:96]
    full = jnp.concatenate([full, jnp.zeros((32, 96), jnp.float32)], axis=1)
    row = lax.broadcasted_iota(jnp.int32, (8, 128), 0)
    lane = lax.broadcasted_iota(jnp.int32, (8, 128), 1)
    moved = jnp.zeros((8, 128), jnp.float32)
    for f in range(2):
        for i in range(COLS):
            at = 16 * f + i // 8 * 8
            tile = jnp.where((row == i % 8) & (lane >= 16 * f) & (lane <= 16 * f + i), full[at : at + 8], 0.0)
            shift = 48 * f + i * (i + 1) // 2
            moved = moved + (pltpu.roll(tile, shift, 1) if shift else tile)
    packed_ref[...] = jnp.broadcast_to(jnp.sum(moved, axis=0, keepdims=True), packed_ref.shape)


def gram(parts, cells, cell_count):
    width = parts.shape[2]
    return pl.pallas_call(
        functools.partial(gram_kernel, cells),
        out_shape=(
            jax.ShapeDtypeStruct((96, width), jnp.bfloat16),
            jax.ShapeDtypeStruct((cell_count, 128), jnp.float32),
        ),
        compiler_params=pltpu.CompilerParams(vmem_limit_bytes=12 << 20),
        name="gram",
    )(parts)


def modes_kernel(rows_total, gram_ref, stack_ref, modes_hbm, triangle_hbm, modes_ref, triangle_ref, entry_ref, left_ref, sem):
    nvar = modes_ref.shape[1]
    cells = modes_ref.shape[3]
    total = jnp.broadcast_to(jnp.sum(gram_ref[...], axis=0, keepdims=True), (128, 128))
    total = jnp.transpose(total)
    entry_ref[...] = jnp.where(lax.broadcasted_iota(jnp.int32, (64, 128), 1) < 64, total[0:64], total[64:128])
    a = {}
    for i in range(COLS):
        for j in range(i + 1):
            a[i, j] = jnp.broadcast_to(entry_ref[pl.ds(i * (i + 1) // 2 + j, 1), :], (8, 128))
    low = {}
    for k in range(COLS):
        inverse = 1.0 / a[k, k]
        for i in range(k + 1, COLS):
            low[i, k] = a[i, k] * inverse
        for i in range(k + 1, COLS):
            for j in range(k + 1, i + 1):
                a[i, j] = a[i, j] - low[i, k] * a[j, k]
    lane = lax.broadcasted_iota(jnp.int32, (8, 128), 1) & 63
    rows = jnp.sqrt(jnp.float32(rows_total))
    shrink = 1.0 / jnp.sqrt(jnp.float32(rows_total * NFFT))
    turned = {}
    for i in range(COLS):
        scale = 1.0 / jnp.sqrt(a[i, i])
        left = jnp.where(lane == i, 1.0, 0.0)
        for j in range(i):
            x = low[i, j]
            for k in range(j + 1, i):
                x = x + low[i, k] * turned[k, j]
            turned[i, j] = -x
            left = jnp.where(lane == j, turned[i, j], left)
        left_ref[2 * i : 2 * i + 2, :] = (left * (scale * rows))[0:2]
        upper = jnp.zeros((8, 128), jnp.float32)
        for k in range(i, COLS):
            upper = jnp.where(lane == k, a[k, i], upper)
        upper = upper * (scale * shrink)
        triangle_ref[i] = jnp.where(
            lax.broadcasted_iota(jnp.int32, (8, 128), 0) == 0, upper, pltpu.roll(upper, 64, 1)
        )[0:2, 0:COLS]
    lane = lax.broadcasted_iota(jnp.int32, (32, 128), 1)
    row = lax.broadcasted_iota(jnp.int32, (32, 128), 0)
    left = left_ref[...]
    left = jnp.where((row & 1) == 0, jnp.where(lane < 16, left, 0.0), jnp.where((lane >= 16) & (lane < 32), pltpu.roll(left, 80, 1), 0.0))
    left = jnp.where(row < 2 * COLS, left, 0.0)
    left = left + pltpu.roll(left, 32, 1) + pltpu.roll(left, 64, 1)
    left = jnp.concatenate([x[:, 0:96] for x in pieces(left)], axis=0)
    copies = [pltpu.make_async_copy(triangle_ref, triangle_hbm, sem.at[nvar])]
    copies[0].start()
    for v in range(nvar):
        x = dot(left, stack_ref[:, v * cells : (v + 1) * cells])
        x = x[64:96] + x[32:64] + x[0:32]
        for j in range(COLS):
            modes_ref[j, v] = x[2 * j : 2 * j + 2, :]
        copies.append(pltpu.make_async_copy(modes_ref.at[:, v], modes_hbm.at[:, v], sem.at[v]))
        copies[-1].start()
    for copy in copies:
        copy.wait()


def modes_of(shares, stack, nvar, cells, cell_count):
    return pl.pallas_call(
        functools.partial(modes_kernel, nvar * cells * cell_count),
        out_shape=(
            jax.ShapeDtypeStruct((COLS, nvar, 2, cells), jnp.float32),
            jax.ShapeDtypeStruct((COLS, 2, COLS), jnp.float32),
        ),
        out_specs=(pl.BlockSpec(memory_space=pltpu.HBM), pl.BlockSpec(memory_space=pltpu.HBM)),
        scratch_shapes=[
            pltpu.VMEM((COLS, nvar, 2, cells), jnp.float32),
            pltpu.VMEM((COLS, 2, COLS), jnp.float32),
            pltpu.VMEM((64, 128), jnp.float32),
            pltpu.VMEM((32, 128), jnp.float32),
            pltpu.SemaphoreType.DMA((nvar + 1,)),
        ],
        compiler_params=pltpu.CompilerParams(vmem_limit_bytes=12 << 20),
        name="modes",
    )(shares, stack)


def chain(snapshots, volumes, freq_index, block_start, exchange, share, cell_count):
    tdev, nvar, cells = snapshots.shape
    parts = exchange(transform(snapshots, volumes, freq_index, block_start))
    stack, packed = gram(parts, cells, cell_count)
    modes, triangle = modes_of(share(packed), stack, nvar, cells, cell_count)
    return jnp.transpose(modes, (2, 0, 1, 3)), jnp.transpose(triangle, (1, 0, 2))


def cell_order(count):
    return [(CELL_FIRST + i) % count for i in range(count)]


def on_device(snapshots, volumes, freq_index, block_start):
    return chain(
        snapshots,
        volumes,
        freq_index,
        block_start,
        lambda x: lax.all_to_all(x, "tm", 0, 0, tiled=True, axis_index_groups=[list(TM_ORDER)]),
        lambda x: lax.all_to_all(x, "cell", 0, 0, tiled=True, axis_index_groups=[cell_order(lax.axis_size("cell"))]),
        lax.axis_size("cell"),
    )


def solution(mesh):
    placed = (P("tm", None, "cell"), P("cell"), P(), P())
    return jax.shard_map(
        on_device,
        mesh=mesh,
        in_specs=placed,
        out_specs=(P("tm", None, None, "cell"), P("tm", None, None)),
        check_vma=False,
    )
```

```python
import functools

import jax
import jax.numpy as jnp
from jax import lax
from jax.experimental import pallas as pl
from jax.experimental.pallas import tpu as pltpu
from jax.sharding import PartitionSpec as P

NFFT = 128
NF = 8
NB = 5
COLS = 2 * NB
SLOTS = NB - 1
TWO_PI = 6.283185307179586
TM_ORDER = (2, 1, 3, 0)
CELL_FIRST = 89


def pieces(x):
    high = x.astype(jnp.bfloat16)
    rest = x - high.astype(jnp.float32)
    middle = rest.astype(jnp.bfloat16)
    low = (rest - middle.astype(jnp.float32)).astype(jnp.bfloat16)
    return high, middle, low


def dot(a, b, contract=((1,), (0,))):
    return lax.dot_general(a, b, (contract, ((), ())), preferred_element_type=jnp.float32)


def transform_kernel(
    freq_hbm, start_hbm, vol_hbm, x_hbm, out_ref, freq_ref, start_ref, vol_ref, x_ref, piece_ref, table_ref, small_sem, in_sem
):
    nvar, tdev, cells = x_hbm.shape

    def incoming(v):
        return pltpu.make_async_copy(x_hbm.at[v], x_ref.at[v], in_sem.at[v])

    small = [
        pltpu.make_async_copy(freq_hbm, freq_ref, small_sem.at[0]),
        pltpu.make_async_copy(start_hbm, start_ref, small_sem.at[1]),
        pltpu.make_async_copy(vol_hbm, vol_ref, small_sem.at[2]),
    ]
    for copy in small:
        copy.start()
    for v in range(nvar):
        incoming(v).start()
    quarter = lax.axis_index("tm")
    first = jnp.where(quarter >= 2, 1, 0)
    sub = lax.broadcasted_iota(jnp.int32, (8, NFFT), 0)
    lane = lax.broadcasted_iota(jnp.int32, (8, NFFT), 1)
    time = lane + quarter * tdev
    turns = jnp.cos(TWO_PI / NFFT * lane.astype(jnp.float32))
    slot = sub % SLOTS
    for copy in small:
        copy.wait()
    start = jnp.zeros((8, NFFT), jnp.int32)
    for s in range(SLOTS):
        start = jnp.where(slot == s, start_ref[first + s], start)
    tau = time - start
    valid = (tau >= 0) & (tau < NFFT)
    hann = jnp.where(valid, 0.5 - 0.5 * jnp.take_along_axis(turns, tau & (NFFT - 1), axis=1), 0.0)
    turn = jnp.where(sub >= SLOTS, NFFT // 4, 0)
    rows = []
    for g in range(NF):
        phase = (freq_ref[2 * TM_ORDER[g // 2] + g % 2] * tau + turn) & (NFFT - 1)
        rows.append((hann * jnp.take_along_axis(turns, phase, axis=1))[:, 0:tdev])
    high, middle, low = pieces(jnp.concatenate(rows, axis=0))
    table_ref[:, 0:tdev] = jnp.concatenate([high, middle, low], axis=0)
    table_ref[:, tdev : 2 * tdev] = jnp.concatenate([high, middle, high], axis=0)
    root = jnp.sqrt(vol_ref[...]).reshape(1, cells)

    def split(v, low):
        rows = slice(low, low + 16)
        x0, x1, x2 = pieces(x_ref[v, rows, :])
        piece_ref[v, low : low + 16, :] = x1
        piece_ref[v, tdev + low : tdev + low + 16, :] = x0
        piece_ref[v, 2 * tdev + low : 2 * tdev + low + 16, :] = x2

    def products(v, low):
        lanes = slice(low, low + 256)
        part = dot(table_ref[128:192], piece_ref[v, tdev : 3 * tdev, lanes])
        total = dot(table_ref[0:128], piece_ref[v, 0 : 2 * tdev, lanes])
        total = (total[0:64] + (total[64:128] + part)) * root[:, lanes]
        out_ref[:, :, v * cells + low : v * cells + low + 256] = total.reshape(4, 16, 256)

    for v in range(nvar):
        incoming(v).wait()
        for low in range(0, tdev, 16):
            split(v, low)
    for low in range(0, cells, 256):
        for v in range(nvar):
            products(v, low)


def transform(snapshots, volumes, freq_index, block_start):
    tdev, nvar, cells = snapshots.shape
    x = jnp.transpose(snapshots, (1, 0, 2))
    return pl.pallas_call(
        transform_kernel,
        out_shape=jax.ShapeDtypeStruct((4, 16, nvar * cells), jnp.float32),
        in_specs=[pl.BlockSpec(memory_space=pltpu.HBM)] * 4,
        out_specs=pl.BlockSpec(memory_space=pltpu.VMEM),
        scratch_shapes=[
            pltpu.SMEM((NF,), jnp.int32),
            pltpu.SMEM((NB,), jnp.int32),
            pltpu.VMEM((cells,), jnp.float32),
            pltpu.VMEM((nvar, tdev, cells), jnp.float32),
            pltpu.VMEM((nvar, 3 * tdev, cells), jnp.bfloat16),
            pltpu.VMEM((192, 2 * tdev), jnp.bfloat16),
            pltpu.SemaphoreType.DMA((3,)),
            pltpu.SemaphoreType.DMA((nvar,)),
        ],
        compiler_params=pltpu.CompilerParams(vmem_limit_bytes=8 << 20),
        name="transform",
    )(*(pltpu.with_memory_space_constraint(a, pltpu.HBM) for a in (freq_index, block_start, volumes, x)))


def gram_kernel(cells, parts_ref, stack_ref, packed_ref):
    sub = lax.broadcasted_iota(jnp.int32, (8, cells), 0)
    full = jnp.zeros((96, 96), jnp.float32)
    place = [TM_ORDER.index(q) for q in range(4)]
    for v in range(parts_ref.shape[2] // cells):
        at = slice(v * cells, (v + 1) * cells)
        tiles = []
        for f in range(2):
            rows = slice(8 * f, 8 * f + 8)
            early = parts_ref[place[0], rows, at] + parts_ref[place[1], rows, at]
            late = parts_ref[place[2], rows, at] + parts_ref[place[3], rows, at]
            early1 = pltpu.roll(early, 1, 0)
            late1 = pltpu.roll(late, 1, 0)
            late2 = pltpu.roll(late, 2, 0)
            upper = jnp.where(sub < 4, early, jnp.where(sub >= 5, early1, 0.0))
            upper = upper + jnp.where((sub >= 1) & (sub < 5), late1, jnp.where(sub >= 6, late2, 0.0))
            lower = jnp.where(sub < 1, early1, 0.0) + jnp.where(sub < 2, late2, 0.0)
            tiles += [upper, lower]
        stack = jnp.concatenate(pieces(jnp.concatenate(tiles, axis=0)), axis=0)
        stack_ref[:, at] = stack
        full = full + dot(stack, stack, ((1,), (1,)))
    full = full[0:32] + full[32:64] + full[64:96]
    full = full[:, 0:32] + full[:, 32:64] + full[:, 64:96]
    full = jnp.concatenate([full, jnp.zeros((32, 96), jnp.float32)], axis=1)
    row = lax.broadcasted_iota(jnp.int32, (8, 128), 0)
    lane = lax.broadcasted_iota(jnp.int32, (8, 128), 1)
    moved = jnp.zeros((8, 128), jnp.float32)
    for f in range(2):
        for i in range(COLS):
            at = 16 * f + i // 8 * 8
            tile = jnp.where((row == i % 8) & (lane >= 16 * f) & (lane <= 16 * f + i), full[at : at + 8], 0.0)
            shift = 48 * f + i * (i + 1) // 2
            moved = moved + (pltpu.roll(tile, shift, 1) if shift else tile)
    packed_ref[...] = jnp.broadcast_to(jnp.sum(moved, axis=0, keepdims=True), packed_ref.shape)


def gram(parts, cells, cell_count):
    width = parts.shape[2]
    return pl.pallas_call(
        functools.partial(gram_kernel, cells),
        out_shape=(
            jax.ShapeDtypeStruct((96, width), jnp.bfloat16),
            jax.ShapeDtypeStruct((cell_count, 128), jnp.float32),
        ),
        compiler_params=pltpu.CompilerParams(vmem_limit_bytes=12 << 20),
        name="gram",
    )(parts)


def modes_kernel(rows_total, gram_ref, stack_ref, modes_hbm, triangle_hbm, modes_ref, triangle_ref, entry_ref, left_ref, sem):
    nvar = modes_ref.shape[1]
    cells = modes_ref.shape[3]
    total = jnp.broadcast_to(jnp.sum(gram_ref[...], axis=0, keepdims=True), (128, 128))
    total = jnp.transpose(total)
    entry_ref[...] = jnp.where(lax.broadcasted_iota(jnp.int32, (64, 128), 1) < 64, total[0:64], total[64:128])
    a = {}
    for i in range(COLS):
        for j in range(i + 1):
            a[i, j] = jnp.broadcast_to(entry_ref[pl.ds(i * (i + 1) // 2 + j, 1), :], (8, 128))
    low = {}
    for k in range(COLS):
        inverse = 1.0 / a[k, k]
        for i in range(k + 1, COLS):
            low[i, k] = a[i, k] * inverse
        for i in range(k + 1, COLS):
            for j in range(k + 1, i + 1):
                a[i, j] = a[i, j] - low[i, k] * a[j, k]
    lane = lax.broadcasted_iota(jnp.int32, (8, 128), 1) & 63
    rows = jnp.sqrt(jnp.float32(rows_total))
    shrink = 1.0 / jnp.sqrt(jnp.float32(rows_total * NFFT))
    turned = {}
    for i in range(COLS):
        scale = 1.0 / jnp.sqrt(a[i, i])
        left = jnp.where(lane == i, 1.0, 0.0)
        for j in range(i):
            x = low[i, j]
            for k in range(j + 1, i):
                x = x + low[i, k] * turned[k, j]
            turned[i, j] = -x
            left = jnp.where(lane == j, turned[i, j], left)
        left_ref[2 * i : 2 * i + 2, :] = (left * (scale * rows))[0:2]
        upper = jnp.zeros((8, 128), jnp.float32)
        for k in range(i, COLS):
            upper = jnp.where(lane == k, a[k, i], upper)
        upper = upper * (scale * shrink)
        triangle_ref[i] = jnp.where(
            lax.broadcasted_iota(jnp.int32, (8, 128), 0) == 0, upper, pltpu.roll(upper, 64, 1)
        )[0:2, 0:COLS]
    lane = lax.broadcasted_iota(jnp.int32, (32, 128), 1)
    row = lax.broadcasted_iota(jnp.int32, (32, 128), 0)
    left = left_ref[...]
    left = jnp.where((row & 1) == 0, jnp.where(lane < 16, left, 0.0), jnp.where((lane >= 16) & (lane < 32), pltpu.roll(left, 80, 1), 0.0))
    left = jnp.where(row < 2 * COLS, left, 0.0)
    left = left + pltpu.roll(left, 32, 1) + pltpu.roll(left, 64, 1)
    left = jnp.concatenate([x[:, 0:96] for x in pieces(left)], axis=0)
    copies = [pltpu.make_async_copy(triangle_ref, triangle_hbm, sem.at[nvar])]
    copies[0].start()
    for v in range(nvar):
        x = dot(left, stack_ref[:, v * cells : (v + 1) * cells])
        x = x[64:96] + x[32:64] + x[0:32]
        for j in range(COLS):
            modes_ref[j, v] = x[2 * j : 2 * j + 2, :]
        copies.append(pltpu.make_async_copy(modes_ref.at[:, v], modes_hbm.at[:, v], sem.at[v]))
        copies[-1].start()
    for copy in copies:
        copy.wait()


def modes_of(shares, stack, nvar, cells, cell_count):
    return pl.pallas_call(
        functools.partial(modes_kernel, nvar * cells * cell_count),
        out_shape=(
            jax.ShapeDtypeStruct((COLS, nvar, 2, cells), jnp.float32),
            jax.ShapeDtypeStruct((COLS, 2, COLS), jnp.float32),
        ),
        out_specs=(pl.BlockSpec(memory_space=pltpu.HBM), pl.BlockSpec(memory_space=pltpu.HBM)),
        scratch_shapes=[
            pltpu.VMEM((COLS, nvar, 2, cells), jnp.float32),
            pltpu.VMEM((COLS, 2, COLS), jnp.float32),
            pltpu.VMEM((64, 128), jnp.float32),
            pltpu.VMEM((32, 128), jnp.float32),
            pltpu.SemaphoreType.DMA((nvar + 1,)),
        ],
        compiler_params=pltpu.CompilerParams(vmem_limit_bytes=12 << 20),
        name="modes",
    )(shares, stack)


def chain(snapshots, volumes, freq_index, block_start, exchange, share, cell_count):
    tdev, nvar, cells = snapshots.shape
    parts = exchange(transform(snapshots, volumes, freq_index, block_start))
    stack, packed = gram(parts, cells, cell_count)
    modes, triangle = modes_of(share(packed), stack, nvar, cells, cell_count)
    return jnp.transpose(modes, (2, 0, 1, 3)), jnp.transpose(triangle, (1, 0, 2))


def cell_order(count):
    return [(CELL_FIRST + i) % count for i in range(count)]


def on_device(snapshots, volumes, freq_index, block_start):
    return chain(
        snapshots,
        volumes,
        freq_index,
        block_start,
        lambda x: lax.all_to_all(x, "tm", 0, 0, tiled=True, axis_index_groups=[list(TM_ORDER)]),
        lambda x: lax.all_to_all(x, "cell", 0, 0, tiled=True, axis_index_groups=[cell_order(lax.axis_size("cell"))]),
        lax.axis_size("cell"),
    )


def solution(mesh):
    placed = (P("tm", None, "cell"), P("cell"), P(), P())
    return jax.shard_map(
        on_device,
        mesh=mesh,
        in_specs=placed,
        out_specs=(P("tm", None, None, "cell"), P("tm", None, None)),
        check_vma=False,
    )
```
